128 devices in a mesh: sec: 2 (over core), dev: 64 (over x, y, z).
Axes of the slice: x: 4, y: 4, z: 4, core: 2. Of those that a mesh axis runs over, the one named last changes fastest.
Arguments:
- field_start: float32 [512, 8, 128, 128], P('dev', None, 'sec'), may hold values from -6 to 6
- forcing: float32 [512, 8, 128, 128], P('dev', None, 'sec'), may hold values from -6 to 6
- traction_start: float32 [128, 65536], P('sec', 'dev'), may hold values from -3 to 3
- conductivity: float32 [512, 8, 128], P('dev'), may hold values from 0.5 to 2
- reaction: float32 [512, 8, 128], P('dev'), may hold values from 0.1 to 2
- surface_order: int32 [65536], P('dev'), may hold values from 0 to 1023, as said below
- near_tiles: bfloat16 [128, 512, 2560], P('dev'), may hold values from -0.125 to 0.125
- col_basis: bfloat16 [128, 32, 512], P('dev'), may hold values from -0.25 to 0.25
- row_basis: bfloat16 [128, 32, 512], P('dev'), may hold values from -1 to 1
- couplings: bfloat16 [128, 32, 4096], P('dev'), may hold values from -0.125 to 0.125
- far_leaf: int32 [128, 128], P('dev'), may hold values from 0 to 1, as said below
Outputs:
- field_end: float32 [512, 8, 128, 128], P('dev', None, 'sec')
- traction_end: float32 [128, 65536], P('sec', 'dev')
The draws below stay inside these ranges and needn't reach their ends.
Inputs may be any that keep to these rules, and one draw needn't show every extreme that they name: `surface_order`: each aligned block of 1024 entries is a permutation of 0 to 1023. `far_leaf`: 0 wherever the row and column clusters lie within 2 of each other.
All inputs are finite; a program needn't handle non-finite values.
Results may differ from the reference program's by a relative error of at most 0.014.
Values may be sent and summed in bfloat16 or wider, within the bound.
No kernel may reach another device: no remote copies, remote signals or barrier semaphores. Data moves between devices by JAX's collectives and lax.ppermute only.
A program may use at most 128 MiB of HBM per device.

```python
import math
import jax
import jax.numpy as jnp
from jax import lax

NY = 8
NZ = 128
R = 128
CLUSTER = 512
RANK = 32
BAND = 2
SWEEPS = 4
BLOCKS = 2
NX = 512
SROW_DEV = 1024
NS = 65536
NCL = 128


def draw_surface_order(key, part):
    slab_keys = jax.random.split(key, NS // SROW_DEV)
    orders = jax.vmap(lambda sub_key: jax.random.permutation(sub_key, SROW_DEV))(slab_keys)
    return orders.reshape(NS).astype(jnp.int32)


def draw_far_leaf(key, part):
    row_ids = jnp.arange(NCL, dtype=jnp.int32)[:, None]
    col_ids = jnp.arange(NCL, dtype=jnp.int32)[None, :]
    density = jax.random.randint(jax.random.fold_in(key, 11), (NCL, 1), 1, 4)
    draws_int = jax.random.randint(jax.random.fold_in(key, 12), (NCL, NCL), 0, 4)
    apart = jnp.abs(row_ids - col_ids) > BAND
    return jnp.where(apart & (draws_int < density), 1, 0).astype(jnp.int32)


def level_of(key, shape, cuts, low, largest):
    factor_of = 1.0
    for position, parts in cuts:
        heights = jax.random.uniform(jax.random.fold_in(jax.random.fold_in(key, 6), position), (parts,), jnp.float32, low / len(cuts), largest / len(cuts))
        factor_of = factor_of * jnp.repeat(jnp.exp(heights), shape[position] // parts).reshape((-1,) + (1,) * (len(shape) - 1 - position))
    return factor_of


def normal_values(key, dims, scale, limit, pieces=(), kind=jnp.bfloat16):
    values = scale * jax.random.normal(key, dims, jnp.float32)
    if pieces:
        values = values * level_of(key, dims, pieces, -0.22, 0.18)
    return jnp.clip(values, -limit, limit).astype(kind)


def setup_inputs(seed: int = 0) -> dict:
    arg_keys = jax.random.split(jax.random.key(seed), 12)
    field_start = normal_values(arg_keys[0], (NX, NY, R, NZ), 1.0, 6.0, ((0, 64), (2, 2)), jnp.float32)
    forcing = normal_values(arg_keys[1], (NX, NY, R, NZ), 1.0, 6.0, ((0, 64), (2, 2)), jnp.float32)
    traction_start = normal_values(arg_keys[2], (R, NS), 0.5, 3.0, ((0, 2), (1, 64)), jnp.float32)
    conductivity = jnp.clip(jnp.exp(math.log(2.0) - 1.3862944 * jax.random.uniform(arg_keys[3], (NX, NY, NZ), jnp.float32) ** level_of(arg_keys[3], (NX, NY, NZ), ((0, 64),), -0.2, 0.2)), 0.5, 2.0)
    reaction = jnp.clip(jnp.exp(math.log(2.0) - 2.9957323 * jax.random.uniform(arg_keys[4], (NX, NY, NZ), jnp.float32) ** level_of(arg_keys[4], (NX, NY, NZ), ((0, 64),), -0.2, 0.2)), 0.1, 2.0)
    surface_order = draw_surface_order(jax.random.fold_in(arg_keys[11], 71), 0)
    near_tiles = normal_values(arg_keys[6], (NCL, CLUSTER, (2 * BAND + 1) * CLUSTER), ((2 * BAND + 1) * CLUSTER) ** -0.5, 0.125, ((0, 64),))
    col_basis = normal_values(arg_keys[7], (NCL, RANK, CLUSTER), CLUSTER ** -0.5, 0.25, ((0, 64),))
    row_basis = normal_values(arg_keys[8], (NCL, RANK, CLUSTER), RANK ** -0.5, 1.0, ((0, 64),))
    couplings = normal_values(arg_keys[9], (NCL, RANK, NCL * RANK), (NCL * RANK // 2) ** -0.5, 0.125, ((0, 64),))
    far_leaf = draw_far_leaf(jax.random.fold_in(arg_keys[11], 71), 0)
    return {"field_start": field_start, "forcing": forcing, "traction_start": traction_start, "conductivity": conductivity, "reaction": reaction, "surface_order": surface_order, "near_tiles": near_tiles, "col_basis": col_basis, "row_basis": row_basis, "couplings": couplings, "far_leaf": far_leaf}


spectrum_center = 1.0
spectrum_half = 0.95


def face_terms(conductivity, reaction):
    padded = jnp.pad(conductivity, 1)
    ny_cells = conductivity.shape[1]
    top_mask = (jnp.arange(ny_cells) < ny_cells - 1).astype(jnp.float32)[None, :, None]
    west_face = 0.5 * (conductivity + padded[:-2, 1:-1, 1:-1])
    east_face = 0.5 * (conductivity + padded[2:, 1:-1, 1:-1])
    south_face = 0.5 * (conductivity + padded[1:-1, :-2, 1:-1])
    north_face = 0.5 * (conductivity + padded[1:-1, 2:, 1:-1]) * top_mask
    lower_face = 0.5 * (conductivity + padded[1:-1, 1:-1, :-2])
    upper_face = 0.5 * (conductivity + padded[1:-1, 1:-1, 2:])
    diagonal = west_face + east_face + south_face + north_face + lower_face + upper_face + reaction
    face_coeffs = tuple(entry[:, :, None, :] for entry in (west_face, east_face, south_face, north_face, lower_face, upper_face))
    return face_coeffs, (1.0 / diagonal)[:, :, None, :], diagonal[:, :, None, :]


def operate(values, face_coeffs, diagonal):
    west_face, east_face, south_face, north_face, lower_face, upper_face = face_coeffs
    padded = jnp.pad(values, ((1, 1), (1, 1), (0, 0), (1, 1)))
    nearby = west_face * padded[:-2, 1:-1, :, 1:-1] + east_face * padded[2:, 1:-1, :, 1:-1]
    nearby = nearby + south_face * padded[1:-1, :-2, :, 1:-1] + north_face * padded[1:-1, 2:, :, 1:-1]
    nearby = nearby + lower_face * padded[1:-1, 1:-1, :, :-2] + upper_face * padded[1:-1, 1:-1, :, 2:]
    return diagonal * values - nearby


def chebyshev(solution, right_side, apply_op, inverse_diag):
    sigma_ratio = spectrum_center / spectrum_half
    residual = right_side - apply_op(solution)
    update = inverse_diag * residual / spectrum_center
    rho_now = 1.0 / sigma_ratio
    for sweep_index in range(SWEEPS):
        solution = solution + update
        if sweep_index + 1 < SWEEPS:
            residual = residual - apply_op(update)
            rho_next = 1.0 / (2.0 * sigma_ratio - rho_now)
            update = (rho_next * rho_now) * update + (2.0 * rho_next / spectrum_half) * (inverse_diag * residual)
            rho_now = rho_next
    return solution


def boundary(traces, near_tiles, col_basis, row_basis, couplings, far_leaf):
    blocks = traces.reshape(R, NCL, CLUSTER)
    padded = jnp.pad(traces, ((0, 0), (BAND * CLUSTER, BAND * CLUSTER)))

    def near_one(pair):
        cluster, tile_rows = pair
        window = lax.dynamic_slice_in_dim(padded, cluster * CLUSTER, (2 * BAND + 1) * CLUSTER, 1)
        return lax.dot_general(window.astype(jnp.float32), tile_rows.astype(jnp.float32), (((1,), (1,)), ((), ())), preferred_element_type=jnp.float32)

    nearby = lax.map(near_one, (jnp.arange(NCL, dtype=jnp.int32), near_tiles))
    nearby = jnp.transpose(nearby, (1, 0, 2)).reshape(R, NS)
    projected = jnp.einsum('nck,crk->ncr', blocks.astype(jnp.float32), col_basis.astype(jnp.float32)).astype(jnp.bfloat16).reshape(R, NCL * RANK)
    leaves = jnp.repeat(far_leaf, RANK, axis=1).astype(couplings.dtype)[:, None, :]
    masked = (couplings * leaves).reshape(NCL * RANK, NCL * RANK)
    coupled = lax.dot_general(projected.astype(jnp.float32), masked.astype(jnp.float32), (((1,), (1,)), ((), ())), preferred_element_type=jnp.float32)
    coupled = coupled.astype(jnp.bfloat16).reshape(R, NCL, RANK)
    distant = jnp.einsum('ncr,crk->nck', coupled.astype(jnp.float32), row_basis.astype(jnp.float32)).reshape(R, NS)
    return nearby + distant


def reference(field_start, forcing, traction_start, conductivity, reaction, surface_order, near_tiles, col_basis, row_basis, couplings, far_leaf):
    face_coeffs, inverse_diag, diagonal = face_terms(conductivity, reaction)
    surface_map = (jnp.arange(NS, dtype=jnp.int32) // SROW_DEV) * SROW_DEV + surface_order.astype(jnp.int32)

    def apply_op(values):
        return operate(values, face_coeffs, diagonal)

    solution = field_start
    traction = traction_start
    for block_index in range(BLOCKS):
        surface = jnp.zeros((R, NX * NZ), jnp.float32).at[:, surface_map].set(traction)
        placed = jnp.transpose(surface.reshape(R, NX, NZ), (1, 0, 2))
        right_side = forcing.at[:, NY - 1, :, :].add(placed)
        solution = chebyshev(solution, right_side, apply_op, inverse_diag)
        top_layer = jnp.transpose(solution[:, NY - 1, :, :], (1, 0, 2)).reshape(R, NX * NZ)
        traces = top_layer[:, surface_map].astype(jnp.bfloat16)
        traction = boundary(traces, near_tiles, col_basis, row_basis, couplings, far_leaf)
    return solution, traction
```

```python
import jax
import jax.numpy as jnp
from jax import lax
from jax.experimental import pallas as pl
from jax.experimental.pallas import tpu as pltpu
from jax.sharding import PartitionSpec as P

CLUSTER = 512
RANK = 32
NDEV = 64
XL = 8
NY = 8
COLS = 64
NZ = 128
SROW = XL * NZ
EXT = XL + 6

f32 = jnp.float32
bf16 = jnp.bfloat16

WEST, EAST, SOUTH, NORTH, LOWER, UPPER = range(6)
NT = (((1,), (1,)), ((), ()))
NN = (((1,), (0,)), ((), ()))


def chebyshev_factors():
    delta = 0.95
    rho = delta
    factors = []
    for _ in range(3):
        following = 1.0 / (2.0 / delta - rho)
        factors.append((following * rho, 2.0 * following / delta))
        rho = following
    return factors


SWAP_A = [(i, i ^ 1) for i in range(NDEV)]
SWAP_B = [(i, i + 1) for i in range(1, NDEV - 1, 2)] + [(i + 1, i) for i in range(1, NDEV - 1, 2)]


def swap(a, b):
    return lax.ppermute(a, "dev", SWAP_A), lax.ppermute(b, "dev", SWAP_B)


def dot(a, b, dims):
    return lax.dot_general(a, b, dims, preferred_element_type=f32)


def faces(c, west, east, reaction):
    iy = lax.broadcasted_iota(jnp.int32, (NY, NZ), 0)
    iz = lax.broadcasted_iota(jnp.int32, (NY, NZ), 1)
    south = jnp.where(iy == 0, 0.0, pltpu.roll(c, 1, 0))
    north = pltpu.roll(c, NY - 1, 0)
    lower = jnp.where(iz == 0, 0.0, pltpu.roll(c, 1, 1))
    upper = jnp.where(iz == NZ - 1, 0.0, pltpu.roll(c, NZ - 1, 1))
    fw = 0.5 * (c + west)
    fe = 0.5 * (c + east)
    fs = 0.5 * (c + south)
    fn = jnp.where(iy == NY - 1, 0.0, 0.5 * (c + north))
    fl = 0.5 * (c + lower)
    fu = 0.5 * (c + upper)
    rest = fs + fn + fl + fu + reaction
    fl = jnp.where(iz == 0, 0.0, fl)
    fu = jnp.where(iz == NZ - 1, 0.0, fu)
    return (fw, fe, fs, fn, fl, fu), rest


def row(coef, kind, e, y):
    return coef[kind, e, y : y + 1, :]


def neighbours(values, west, here, east, coef, e, y):
    v = values[here, y]
    acc = row(coef, WEST, e, y) * values[west, y] + row(coef, EAST, e, y) * values[east, y]
    acc = acc + row(coef, LOWER, e, y) * pltpu.roll(v, 1, 1)
    acc = acc + row(coef, UPPER, e, y) * pltpu.roll(v, NZ - 1, 1)
    if y > 0:
        acc = acc + row(coef, SOUTH, e, y) * values[here, y - 1]
    if y < NY - 1:
        acc = acc + row(coef, NORTH, e, y) * values[here, y + 1]
    return v, acc


def build_onehot(order, onehot):
    wanted = order[...]
    for x in range(XL):
        cell = lax.broadcasted_iota(jnp.int32, (NZ, SROW), 0) + x * NZ
        onehot[x * NZ : (x + 1) * NZ, :] = jnp.where(cell == wanted, 1.0, 0.0).astype(bf16)


def place(traction, onehot):
    high = traction.astype(bf16)
    low = (traction - high.astype(f32)).astype(bf16)
    both = dot(jnp.concatenate([high, low], axis=0), onehot[...], NT)
    return both[:COLS] + both[COLS:]


def residual(values, forcing, cond, reac, raw, out, placed):
    for x in range(XL):
        c = cond[x]
        zero = jnp.zeros_like(c)
        west = cond[x - 1] if x > 0 else zero
        east = cond[x + 1] if x < XL - 1 else zero
        sides, rest = faces(c, west, east, reac[x])
        sides = list(sides)
        if x == 0:
            sides[WEST] = zero
        if x == XL - 1:
            sides[EAST] = zero
        for kind in range(6):
            raw[kind, x] = sides[kind]
        raw[6, x] = rest + sides[WEST] + sides[EAST]

    def layer(x, carry):
        west = jnp.maximum(x - 1, 0)
        east = jnp.minimum(x + 1, XL - 1)
        for y in range(NY):
            v, acc = neighbours(values, west, x, east, raw, x, y)
            res = forcing[x, y] + acc - row(raw, 6, x, y) * v
            if placed is not None and y == NY - 1:
                res = res + placed[x]
            out[x, y] = res
        return carry

    lax.fori_loop(0, XL, layer, 0)


def pack(odd, values, res, cond, reac, send_a, send_b, with_coef):
    for send, toward_right in ((send_a, odd == 0), (send_b, odd != 0)):

        def source(h):
            return jnp.where(toward_right, XL - h, h - 1)

        def copy(y, carry):
            send[y] = values[source(1), y].astype(bf16)
            for h in (1, 2, 3):
                send[h * NY + y] = res[source(h), y].astype(bf16)
            return carry

        lax.fori_loop(0, NY, copy, 0)
        if with_coef:
            rows = [cond[source(h)] for h in (1, 2, 3, 4)] + [reac[source(h)] for h in (1, 2, 3)]
            rows.append(jnp.zeros_like(rows[0]))
            send[4 * NY] = jnp.concatenate(rows, axis=0).astype(bf16)


def first_kernel(
    scal, values, forcing, traction, order, cond, reac, res, send_a, send_b, raw, onehot, placed
):
    build_onehot(order, onehot)
    cells = place(traction[...], onehot)
    for x in range(XL):
        placed[x] = cells[:, x * NZ : (x + 1) * NZ]
    residual(values, forcing, cond, reac, raw, res, placed)
    pack(scal[0], values, res, cond, reac, send_a, send_b, True)


def second_kernel(scal, values, forcing, cond, reac, res, send_a, send_b, raw):
    residual(values, forcing, cond, reac, raw, res, None)
    pack(scal[0], values, res, cond, reac, send_a, send_b, False)


def sides_of(odd, recv_a, recv_b):
    return ((recv_a, odd == 0), (recv_b, odd != 0))


def coefficients(scal, recv_a, recv_b, cond, reac, cond_ext, reac_ext, coef, inv):
    odd = scal[0]
    for x in range(XL):
        cond_ext[x + 4] = cond[x]
        reac_ext[x + 3] = reac[x]
    for recv, right in sides_of(odd, recv_a, recv_b):
        rows = recv[4 * NY].astype(f32)
        for h in (1, 2, 3, 4):
            cond_ext[jnp.where(right, 11 + h, 4 - h)] = rows[(h - 1) * NY : h * NY]
        for h in (1, 2, 3):
            reac_ext[jnp.where(right, 10 + h, 3 - h)] = rows[(h + 3) * NY : (h + 4) * NY]
    for e in range(EXT):
        sides, rest = faces(cond_ext[e + 1], cond_ext[e], cond_ext[e + 2], reac_ext[e])
        diagonal = rest + sides[WEST] + sides[EAST]
        scale = 1.0 / jnp.where(diagonal > 0.0, diagonal, 1.0)
        if e < 3:
            scale = jnp.where(scal[1] > 0, scale, 0.0)
        if e >= XL + 3:
            scale = jnp.where(scal[2] > 0, scale, 0.0)
        for kind in range(6):
            coef[kind, e] = sides[kind] * scale
        inv[e] = scale


def start_of_sweeps(odd, values, res, recv_a, recv_b, coef, inv, first, placed, tract_a, tract_b):
    def own(x, carry):
        for y in range(NY):
            r = res[x, y]
            if placed is not None and y == NY - 1:
                r = r + placed[x]
            first[x + 3, y] = r * inv[x + 3, y : y + 1, :]
        return carry

    lax.fori_loop(0, XL, own, 0)
    for (recv, right), tract in zip(sides_of(odd, recv_a, recv_b), (tract_a, tract_b)):
        edge = jnp.where(right, XL - 1, 0)
        toward = jnp.where(right, EAST, WEST)
        back = jnp.where(right, WEST, EAST)

        def halo(h):
            return jnp.where(right, XL + 2 + h, 3 - h)

        for y in range(NY):
            gap = recv[y].astype(f32) - values[edge, y]
            e = edge + 3
            first[e, y] = first[e, y] + row(coef, toward, e, y) * gap
            for h in (1, 2, 3):
                e = halo(h)
                r = recv[h * NY + y].astype(f32)
                if tract is not None and y == NY - 1:
                    r = r + tract[h - 1].astype(f32)
                s = r * inv[e, y : y + 1, :]
                if h == 1:
                    s = s - row(coef, back, e, y) * gap
                first[e, y] = s


def sweeps(values, coef, first, second, third, out):
    (a1, b1), (a2, b2), (a3, b3) = chebyshev_factors()

    def step_2(e, carry):
        for y in range(NY):
            v, acc = neighbours(first, e - 1, e, e + 1, coef, e, y)
            second[e, y] = (1.0 + a1) * v + b1 * acc
        return carry

    def step_3(e, carry):
        for y in range(NY):
            v, acc = neighbours(second, e - 1, e, e + 1, coef, e, y)
            third[e, y] = (1.0 + a2 - b2) * v + (b2 - a2) * first[e, y] + b2 * acc
        return carry

    def step_4(e, carry):
        for y in range(NY):
            v, acc = neighbours(third, e - 1, e, e + 1, coef, e, y)
            d = (1.0 + a3 - b3) * v - a3 * second[e, y] + b3 * (first[e, y] + acc)
            out[e - 3, y] = values[e - 3, y] + d
        return carry

    lax.fori_loop(1, EXT - 1, step_2, 0)
    lax.fori_loop(2, EXT - 2, step_3, 0)
    lax.fori_loop(3, EXT - 3, step_4, 0)


def surface(out, order, col_basis, onehot, traces, spread):
    build_onehot(order, onehot)
    top = jnp.concatenate([out[x, NY - 1] for x in range(XL)], axis=1).astype(bf16)
    tr = dot(top, onehot[...], NN).astype(bf16)
    traces[...] = tr
    parts = [
        dot(col_basis[c], tr[:, c * CLUSTER : (c + 1) * CLUSTER], NT) for c in range(2)
    ]
    packed = jnp.concatenate(parts, axis=1).astype(bf16)

    def copy(i, carry):
        spread[i] = packed
        return carry

    lax.fori_loop(0, NDEV, copy, 0)


def sweep_1_kernel(
    scal, values, res, recv_a, recv_b, cond, reac, order, col_basis,
    out, traces, spread, coef, inv,
    cond_ext, reac_ext, first, second, third, onehot,
):
    coefficients(scal, recv_a, recv_b, cond, reac, cond_ext, reac_ext, coef, inv)
    start_of_sweeps(scal[0], values, res, recv_a, recv_b, coef, inv, first, None, None, None)
    sweeps(values, coef, first, second, third, out)
    surface(out, order, col_basis, onehot, traces, spread)


def sweep_2_kernel(
    scal, values, res, recv_a, recv_b, placed, tract_a, tract_b, order, col_basis, coef, inv,
    out, traces, spread,
    first, second, third, onehot,
):
    start_of_sweeps(
        scal[0], values, res, recv_a, recv_b, coef, inv, first, placed, tract_a, tract_b
    )
    sweeps(values, coef, first, second, third, out)
    surface(out, order, col_basis, onehot, traces, spread)


def mask_kernel(couplings, leaf, masked):
    wide = NDEV * 2 * RANK
    cluster = lax.broadcasted_iota(jnp.int32, (NDEV * 2, wide), 0)
    lane = lax.broadcasted_iota(jnp.int32, (NDEV * 2, wide), 1)
    spread = jnp.where(lane // RANK == cluster, 1.0, 0.0).astype(bf16)
    for c in range(2):
        flags = jnp.broadcast_to(leaf[c : c + 1, :].astype(f32), (16, NDEV * 2)).astype(bf16)
        weights = dot(flags, spread, NN)[0:1]
        rows = couplings[c * RANK : (c + 1) * RANK, :].astype(f32)
        masked[c * RANK : (c + 1) * RANK, :] = (rows * weights).astype(bf16)


def near_kernel(scal, traces, recv_a, recv_b, tiles, out, window):
    odd = scal[0]
    window[1] = traces[...]
    for recv, right in sides_of(odd, recv_a, recv_b):
        window[jnp.where(right, 2, 0)] = recv[...]
    half = CLUSTER
    acc = dot(window[0], tiles[0, :, : 2 * half], NT)
    acc = acc + dot(window[1], tiles[0, :, 2 * half : 4 * half], NT)
    acc = acc + dot(window[2, :, :half], tiles[0, :, 4 * half :], NT)
    out[:, :half] = acc
    acc = dot(window[0, :, half:], tiles[1, :, :half], NT)
    acc = acc + dot(window[1], tiles[1, :, half : 3 * half], NT)
    acc = acc + dot(window[2], tiles[1, :, 3 * half :], NT)
    out[:, half:] = acc


def far_part(gathered, masked, row_basis, nearby, out):
    g = gathered[...]
    turned = jnp.concatenate([g[:, :, COLS:], g[:, :, :COLS]], axis=2)
    g = jnp.concatenate([g, turned], axis=1).reshape(NDEV * 2 * RANK, NZ)
    coupled = dot(masked[...], g, NN)
    coupled = jnp.transpose(coupled)[:COLS].astype(bf16)
    for c in range(2):
        cut = slice(c * CLUSTER, (c + 1) * CLUSTER)
        part = dot(coupled[:, c * RANK : (c + 1) * RANK], row_basis[c], NN)
        out[:, cut] = nearby[:, cut] + part


def far_kernel_place(
    scal, gathered, masked, row_basis, nearby, order, placed, send_a, send_b, onehot, total
):
    far_part(gathered, masked, row_basis, nearby, total)
    build_onehot(order, onehot)
    cells = place(total[...], onehot)
    for x in range(XL):
        placed[x] = cells[:, x * NZ : (x + 1) * NZ]
    for send, right in ((send_a, scal[0] == 0), (send_b, scal[0] != 0)):
        for h in (1, 2, 3):
            send[h - 1] = placed[jnp.where(right, XL - h, h - 1)].astype(bf16)


def far_kernel_last(gathered, masked, row_basis, nearby, out):
    far_part(gathered, masked, row_basis, nearby, out)


def struct(shape, dtype):
    return jax.ShapeDtypeStruct(shape, dtype)


def call(kernel, outs, scratch, *operands, scalars=None):
    specs = [pl.BlockSpec() for _ in operands]
    if scalars is not None:
        specs = [pl.BlockSpec(memory_space=pltpu.SMEM)] + specs
        operands = (scalars,) + operands
    return pl.pallas_call(
        kernel,
        out_shape=outs,
        in_specs=specs,
        out_specs=jax.tree.map(lambda _: pl.BlockSpec(), outs),
        scratch_shapes=scratch,
        compiler_params=pltpu.CompilerParams(vmem_limit_bytes=56 << 20),
        name=kernel.__name__,
    )(*operands)


FIELD = (XL, NY, COLS, NZ)
EXT_FIELD = pltpu.VMEM((EXT, NY, COLS, NZ), f32)
ONEHOT = pltpu.VMEM((SROW, SROW), bf16)
RAW = pltpu.VMEM((7, XL, NY, NZ), f32)


def exchange_boundary(scal, traces, spread, tiles):
    near_a, near_b = swap(traces, traces)
    gathered = lax.all_to_all(spread, "dev", split_axis=0, concat_axis=0, tiled=True)
    nearby = call(
        near_kernel,
        struct((COLS, SROW), f32),
        [pltpu.VMEM((3, COLS, SROW), bf16)],
        traces, near_a, near_b, tiles,
        scalars=scal,
    )
    return gathered, nearby


def shards(
    field_start, forcing, traction_start, conductivity, reaction, surface_order,
    near_tiles, col_basis, row_basis, couplings, far_leaf,
):
    index = lax.axis_index("dev").astype(jnp.int32)
    scal = jnp.stack(
        [index % 2, (index > 0).astype(jnp.int32), (index < NDEV - 1).astype(jnp.int32)]
    )
    order = surface_order.reshape(1, SROW)
    message = struct((4 * NY + 1, COLS, NZ), bf16)
    res, send_a, send_b = call(
        first_kernel,
        (struct(FIELD, f32), message, message),
        [RAW, ONEHOT, pltpu.VMEM((XL, COLS, NZ), f32)],
        field_start, forcing, traction_start, order, conductivity, reaction,
        scalars=scal,
    )
    recv_a, recv_b = swap(send_a, send_b)
    masked = call(
        mask_kernel,
        struct((2 * RANK, NDEV * 2 * RANK), bf16),
        [],
        couplings.reshape(2 * RANK, NDEV * 2 * RANK), far_leaf,
    )
    coef_shape = struct((6, EXT, NY, NZ), f32)
    inv_shape = struct((EXT, NY, NZ), f32)
    surface_outs = (
        struct(FIELD, f32), struct((COLS, SROW), bf16), struct((NDEV, RANK, NZ), bf16),
    )
    field, traces, spread, coef, inv = call(
        sweep_1_kernel,
        surface_outs + (coef_shape, inv_shape),
        [
            pltpu.VMEM((XL + 8, NY, NZ), f32), pltpu.VMEM((EXT, NY, NZ), f32),
            EXT_FIELD, EXT_FIELD, EXT_FIELD, ONEHOT,
        ],
        field_start, res, recv_a, recv_b, conductivity, reaction, order, col_basis,
        scalars=scal,
    )
    gathered, nearby = exchange_boundary(scal, traces, spread, near_tiles)
    message = struct((4 * NY, COLS, NZ), bf16)
    res, send_a, send_b = call(
        second_kernel,
        (struct(FIELD, f32), message, message),
        [RAW],
        field, forcing, conductivity, reaction,
        scalars=scal,
    )
    recv_a, recv_b = swap(send_a, send_b)
    tract = struct((3, COLS, NZ), bf16)
    placed, send_a, send_b = call(
        far_kernel_place,
        (struct((XL, COLS, NZ), f32), tract, tract),
        [ONEHOT, pltpu.VMEM((COLS, SROW), f32)],
        gathered, masked, row_basis, nearby, order,
        scalars=scal,
    )
    tract_a, tract_b = swap(send_a, send_b)
    field, traces, spread = call(
        sweep_2_kernel,
        surface_outs,
        [EXT_FIELD, EXT_FIELD, EXT_FIELD, ONEHOT],
        field, res, recv_a, recv_b, placed, tract_a, tract_b, order, col_basis, coef, inv,
        scalars=scal,
    )
    gathered, nearby = exchange_boundary(scal, traces, spread, near_tiles)
    traction = call(
        far_kernel_last,
        struct((COLS, SROW), f32),
        [],
        gathered, masked, row_basis, nearby,
    )
    return field, traction


def solution(mesh):
    in_specs = (
        P("dev", None, "sec", None),
        P("dev", None, "sec", None),
        P("sec", "dev"),
        P("dev", None, None),
        P("dev", None, None),
        P("dev"),
        P("dev", None, None),
        P("dev", None, None),
        P("dev", None, None),
        P("dev", None, None),
        P("dev", None),
    )
    out_specs = (P("dev", None, "sec", None), P("sec", "dev"))
    return jax.shard_map(shards, mesh=mesh, in_specs=in_specs, out_specs=out_specs, check_vma=False)
```

```python
import jax
import jax.numpy as jnp
from jax import lax
from jax.experimental import pallas as pl
from jax.experimental.pallas import tpu as pltpu
from jax.sharding import PartitionSpec as P


CLUSTER = 512
RANK = 32
NDEV = 64
XL = 8
NY = 8
COLS = 64
NZ = 128
SROW = XL * NZ
EXT = XL + 6

f32 = jnp.float32
bf16 = jnp.bfloat16

WEST, EAST, SOUTH, NORTH, LOWER, UPPER = range(6)
NT = (((1,), (1,)), ((), ()))
NN = (((1,), (0,)), ((), ()))


def chebyshev_factors():
    delta = 0.95
    rho = delta
    factors = []
    for _ in range(3):
        following = 1.0 / (2.0 / delta - rho)
        factors.append((following * rho, 2.0 * following / delta))
        rho = following
    return factors


SWAP_A = [(i, i ^ 1) for i in range(NDEV)]
SWAP_B = [(i, i + 1) for i in range(1, NDEV - 1, 2)] + [(i + 1, i) for i in range(1, NDEV - 1, 2)]


def swap(a, b):
    return lax.ppermute(a, "dev", SWAP_A), lax.ppermute(b, "dev", SWAP_B)


def dot(a, b, dims):
    return lax.dot_general(a, b, dims, preferred_element_type=f32)


def faces(c, west, east, reaction):
    iy = lax.broadcasted_iota(jnp.int32, (NY, NZ), 0)
    iz = lax.broadcasted_iota(jnp.int32, (NY, NZ), 1)
    south = jnp.where(iy == 0, 0.0, pltpu.roll(c, 1, 0))
    north = pltpu.roll(c, NY - 1, 0)
    lower = jnp.where(iz == 0, 0.0, pltpu.roll(c, 1, 1))
    upper = jnp.where(iz == NZ - 1, 0.0, pltpu.roll(c, NZ - 1, 1))
    fw = 0.5 * (c + west)
    fe = 0.5 * (c + east)
    fs = 0.5 * (c + south)
    fn = jnp.where(iy == NY - 1, 0.0, 0.5 * (c + north))
    fl = 0.5 * (c + lower)
    fu = 0.5 * (c + upper)
    rest = fs + fn + fl + fu + reaction
    fl = jnp.where(iz == 0, 0.0, fl)
    fu = jnp.where(iz == NZ - 1, 0.0, fu)
    return (fw, fe, fs, fn, fl, fu), rest


def row(coef, kind, e, y):
    return coef[kind, e, y : y + 1, :]


def tile(values, e, y):
    return values[e, y].reshape(COLS // 8, 8, NZ)


def put(out, e, y, value):
    out[e, y] = value.reshape(COLS, NZ)


def neighbours(values, west, here, east, coef, e, y):
    v = tile(values, here, y)
    acc = row(coef, WEST, e, y) * tile(values, west, y)
    acc = acc + row(coef, EAST, e, y) * tile(values, east, y)
    acc = acc + row(coef, LOWER, e, y) * pltpu.roll(v, 1, 2)
    acc = acc + row(coef, UPPER, e, y) * pltpu.roll(v, NZ - 1, 2)
    if y > 0:
        acc = acc + row(coef, SOUTH, e, y) * tile(values, here, y - 1)
    if y < NY - 1:
        acc = acc + row(coef, NORTH, e, y) * tile(values, here, y + 1)
    return v, acc


def build_onehot(order, onehot):
    wanted = order[...]

    def rows(x, carry):
        cell = lax.broadcasted_iota(jnp.int32, (NZ, SROW), 0) + x * NZ
        onehot[pl.ds(pl.multiple_of(x * NZ, NZ), NZ), :] = jnp.where(
            cell == wanted, 1.0, 0.0
        ).astype(bf16)
        return carry

    lax.fori_loop(0, XL, rows, 0)


def place(traction, onehot):
    high = traction.astype(bf16)
    low = (traction - high.astype(f32)).astype(bf16)
    both = dot(jnp.concatenate([high, low], axis=0), onehot[...], NT)
    return both[:COLS] + both[COLS:]


def raw_faces(cond, reac, raw):
    def layer(x, carry):
        sides, rest = faces(
            cond[x], cond[jnp.maximum(x - 1, 0)], cond[jnp.minimum(x + 1, XL - 1)], reac[x]
        )
        sides = list(sides)
        sides[WEST] = jnp.where(x == 0, 0.0, sides[WEST])
        sides[EAST] = jnp.where(x == XL - 1, 0.0, sides[EAST])
        for kind in range(6):
            raw[kind, x] = sides[kind]
        raw[6, x] = rest + sides[WEST] + sides[EAST]
        return carry

    lax.fori_loop(0, XL, layer, 0, unroll=8)


def residual_layer(x, values, forcing, raw, out, placed):
    west = jnp.maximum(x - 1, 0)
    east = jnp.minimum(x + 1, XL - 1)
    for y in range(NY):
        v, acc = neighbours(values, west, x, east, raw, x, y)
        res = tile(forcing, x, y) + acc - row(raw, 6, x, y) * v
        if placed is not None and y == NY - 1:
            res = res + placed[x].reshape(COLS // 8, 8, NZ)
        put(out, x, y, res)


def pack(odd, values, res, sends_near, sends_far, base):
    for near, far, right in zip(sends_near, sends_far, (odd == 0, odd != 0)):

        def source(h):
            return jnp.where(right, XL - h, h - 1)

        def copy(y, carry):
            near[y] = values[source(1), y].astype(bf16)
            near[NY + y] = res[source(1), y].astype(bf16)
            for h in (2, 3):
                far[base + (h - 2) * NY + y] = res[source(h), y].astype(bf16)
            return carry

        lax.fori_loop(0, NY, copy, 0, unroll=2)


def pack_coefficients(odd, cond, reac, send_a, send_b):
    for send, right in ((send_a, odd == 0), (send_b, odd != 0)):

        def source(h):
            return jnp.where(right, XL - h, h - 1)

        rows = [cond[source(h)] for h in (1, 2, 3, 4)] + [reac[source(h)] for h in (1, 2, 3)]
        rows.append(jnp.zeros_like(rows[0]))
        send[2 * NY] = jnp.concatenate(rows, axis=0).astype(bf16)


def position():
    index = lax.axis_index("dev")
    return index, lax.rem(index, 2)


def first_kernel(
    values_hbm, forcing_hbm, traction_hbm, order_hbm, cond_hbm, reac_hbm,
    values, forcing, cond, reac, res, send_a, send_b, far_a, far_b,
    order, traction, raw, onehot, placed, small_sems, sems,
):
    _, odd = position()
    small = [
        pltpu.make_async_copy(source, target, small_sems.at[i])
        for i, (source, target) in enumerate(
            ((order_hbm, order), (traction_hbm, traction), (cond_hbm, cond), (reac_hbm, reac))
        )
    ]
    for copy in small:
        copy.start()

    def layer_copies(x):
        return (
            pltpu.make_async_copy(values_hbm.at[x], values.at[x], sems.at[0, x]),
            pltpu.make_async_copy(forcing_hbm.at[x], forcing.at[x], sems.at[1, x]),
        )

    for x in range(XL):
        for copy in layer_copies(x):
            copy.start()
    small[0].wait()
    build_onehot(order, onehot)
    small[1].wait()
    cells = place(traction[...], onehot)
    for x in range(XL):
        placed[x] = cells[:, x * NZ : (x + 1) * NZ]
    small[2].wait()
    small[3].wait()
    raw_faces(cond, reac, raw)
    pack_coefficients(odd, cond, reac, send_a, send_b)
    for copy in layer_copies(0):
        copy.wait()

    def layer(x, carry):
        @pl.when(x < XL - 1)
        def _():
            for copy in layer_copies(x + 1):
                copy.wait()

        residual_layer(x, values, forcing, raw, res, placed)
        return carry

    lax.fori_loop(0, XL, layer, 0)
    pack(odd, values, res, (send_a, send_b), (far_a, far_b), 0)


def sides_of(odd, recv_a, recv_b):
    return ((recv_a, odd == 0), (recv_b, odd != 0))


def extend(odd, recv_a, recv_b, cond, reac, cond_ext, reac_ext):
    for x in range(XL):
        cond_ext[x + 4] = cond[x]
        reac_ext[x + 3] = reac[x]
    for recv, right in sides_of(odd, recv_a, recv_b):
        rows = recv[2 * NY].astype(f32)
        for h in (1, 2, 3, 4):
            cond_ext[jnp.where(right, 11 + h, 4 - h)] = rows[(h - 1) * NY : h * NY]
        for h in (1, 2, 3):
            reac_ext[jnp.where(right, 10 + h, 3 - h)] = rows[(h + 3) * NY : (h + 4) * NY]


def normalise(index, cond_ext, reac_ext, coef, inv):

    def layer(e, carry):
        sides, rest = faces(cond_ext[e + 1], cond_ext[e], cond_ext[e + 2], reac_ext[e])
        diagonal = rest + sides[WEST] + sides[EAST]
        scale = 1.0 / jnp.where(diagonal > 0.0, diagonal, 1.0)
        outside = ((index == 0) & (e < 3)) | ((index == NDEV - 1) & (e >= XL + 3))
        scale = jnp.where(outside, 0.0, scale)
        for kind in range(6):
            coef[kind, e] = sides[kind] * scale
        inv[0, e] = scale
        return carry

    lax.fori_loop(0, EXT, layer, 0, unroll=7)


def widen(value):
    return value.astype(f32).reshape(COLS // 8, 8, NZ)


def start_own(odd, values, res, recv_a, recv_b, coef, inv, first, placed):
    def own(x, carry):
        for y in range(NY):
            r = tile(res, x, y)
            if placed is not None and y == NY - 1:
                r = r + placed[x].reshape(COLS // 8, 8, NZ)
            put(first, x + 3, y, r * row(inv, 0, x + 3, y))
        return carry

    lax.fori_loop(0, XL, own, 0, unroll=2)
    for recv, right in sides_of(odd, recv_a, recv_b):
        edge = jnp.where(right, XL - 1, 0)
        toward = jnp.where(right, EAST, WEST)
        e = edge + 3
        for y in range(NY):
            gap = widen(recv[y]) - tile(values, edge, y)
            put(first, e, y, tile(first, e, y) + row(coef, toward, e, y) * gap)


def start_halo(h, odd, values, recvs, far, coef, inv, first, tracts):
    messages, base = far
    for side, right in enumerate((odd == 0, odd != 0)):
        edge = jnp.where(right, XL - 1, 0)
        back = jnp.where(right, WEST, EAST)
        e = jnp.where(right, XL + 2 + h, 3 - h)
        for y in range(NY):
            if h == 1:
                r = widen(recvs[side][NY + y])
            else:
                r = widen(messages[side][base + (h - 2) * NY + y])
            if tracts is not None and y == NY - 1:
                r = r + widen(tracts[side][h - 1])
            s = r * row(inv, 0, e, y)
            if h == 1:
                gap = widen(recvs[side][y]) - tile(values, edge, y)
                s = s - row(coef, back, e, y) * gap
            put(first, e, y, s)


def sweeps(known, values, coef, first, second, third, out):
    (a1, b1), (a2, b2), (a3, b3) = chebyshev_factors()

    def step_2(e):
        for y in range(NY):
            v, acc = neighbours(first, e - 1, e, e + 1, coef, e, y)
            put(second, e, y, ((1.0 + a1) / b1) * v + acc)

    def step_3(e):
        for y in range(NY):
            v, acc = neighbours(second, e - 1, e, e + 1, coef, e, y)
            s = tile(first, e, y)
            put(third, e, y, ((1.0 + a2 - b2) / b2) * v + ((b2 - a2) / (b1 * b2)) * s + acc)

    def step_4(e):
        for y in range(NY):
            v, acc = neighbours(third, e - 1, e, e + 1, coef, e, y)
            d = ((1.0 + a3 - b3) / b3) * v - (a3 / (b2 * b3)) * tile(second, e, y) + acc
            d = (b1 * b2 * b3) * d + b3 * tile(first, e, y)
            put(out, e - 3, y, tile(values, e - 3, y) + d)

    for level, step in ((1, step_2), (2, step_3), (3, step_4)):
        low, high = 3 + level - known[0], XL + 3 - level + known[0]

        if known[1]:
            left = low - level

            def later(i, carry):
                step(jnp.where(i < left, level + i, high + i - left))
                return carry

            lax.fori_loop(0, 2 * left, later, 0, unroll=2)
        else:

            def now(e, carry):
                step(e)
                return carry

            lax.fori_loop(low, high, now, 0, unroll=2)


def surface(out, order, col_basis, onehot, traces, spread):
    build_onehot(order, onehot)
    top = jnp.concatenate([out[x, NY - 1] for x in range(XL)], axis=1).astype(bf16)
    tr = dot(top, onehot[...], NN).astype(bf16)
    traces[...] = tr
    parts = [
        dot(col_basis[c], tr[:, c * CLUSTER : (c + 1) * CLUSTER], NT) for c in range(2)
    ]
    packed = jnp.concatenate(parts, axis=1).astype(bf16)

    def copy(i, carry):
        spread[i] = packed
        return carry

    lax.fori_loop(0, NDEV, copy, 0, unroll=8)


BLOCK_1 = 1
BLOCK_2 = 0


def sweep_1a_kernel(
    values, cond, reac, res, recv_a, recv_b,
    cond_ext, reac_ext, coef, inv, first, second, third, out,
):
    index, odd = position()
    extend(odd, recv_a, recv_b, cond, reac, cond_ext, reac_ext)
    normalise(index, cond_ext, reac_ext, coef, inv)
    start_own(odd, values, res, recv_a, recv_b, coef, inv, first, None)
    start_halo(1, odd, values, (recv_a, recv_b), (None, 0), coef, inv, first, None)
    sweeps((BLOCK_1, False), values, coef, first, second, third, out)


def sweep_1b_kernel(
    values, forcing, cond, reac, far_a, far_b, coef, inv, order, col_basis,
    first_in, second_in, third_in, out_in,
    out_hbm, res_hbm, traces, send_a, send_b, spread, first, second, third, out,
    raw, onehot, sems,
):
    _, odd = position()
    for h in (2, 3):
        start_halo(h, odd, values, None, ((far_a, far_b), 0), coef, inv, first, None)
    sweeps((BLOCK_1, True), values, coef, first, second, third, out)
    out_copy = pltpu.make_async_copy(out, out_hbm, sems.at[0])
    out_copy.start()
    surface(out, order, col_basis, onehot, traces, spread)
    raw_faces(cond, reac, raw)

    def layer(x, carry):
        residual_layer(x, out, forcing, raw, second, None)
        return carry

    lax.fori_loop(0, XL, layer, 0, unroll=2)
    res_copy = pltpu.make_async_copy(second.at[pl.ds(0, XL)], res_hbm, sems.at[1])
    res_copy.start()
    pack(odd, out, second, (send_a, send_b), (send_a, send_b), 2 * NY)
    out_copy.wait()
    res_copy.wait()


def sweep_2a_kernel(
    values_hbm, res, cond_ext, reac_ext, recv_a, recv_b, placed,
    values, coef, inv, first, second, third, out,
    sems,
):
    index, odd = position()
    inner = pl.ds(1, XL - 2)
    loads = [
        pltpu.make_async_copy(values_hbm.at[x], values.at[x], sems.at[i])
        for i, x in enumerate((0, XL - 1))
    ]
    loads.append(pltpu.make_async_copy(values_hbm.at[inner], values.at[inner], sems.at[2]))
    for load in loads:
        load.start()
    normalise(index, cond_ext, reac_ext, coef, inv)
    for load in loads:
        load.wait()
    start_own(odd, values, res, recv_a, recv_b, coef, inv, first, placed)
    sweeps((BLOCK_2, False), values, coef, first, second, third, out)


def sweep_2b_kernel(
    values, recv_a, recv_b, tract_a, tract_b, coef, inv, order, col_basis,
    first_in, second_in, third_in, out_in,
    out_hbm, traces, spread, first, second, third, out,
    onehot, sem,
):
    _, odd = position()
    recvs = (recv_a, recv_b)
    for h in (1, 2, 3):
        start_halo(
            h, odd, values, recvs, (recvs, 2 * NY), coef, inv, first, (tract_a, tract_b)
        )
    sweeps((BLOCK_2, True), values, coef, first, second, third, out)
    out_copy = pltpu.make_async_copy(out, out_hbm, sem)
    out_copy.start()
    surface(out, order, col_basis, onehot, traces, spread)
    out_copy.wait()


def mask_kernel(couplings, leaf, masked):
    wide = NDEV * 2 * RANK
    cluster = lax.broadcasted_iota(jnp.int32, (NDEV * 2, wide), 0)
    lane = lax.broadcasted_iota(jnp.int32, (NDEV * 2, wide), 1)
    spread = jnp.where(lane // RANK == cluster, 1.0, 0.0).astype(bf16)
    for c in range(2):
        flags = jnp.broadcast_to(leaf[c : c + 1, :].astype(f32), (16, NDEV * 2)).astype(bf16)
        weights = dot(flags, spread, NN)[0:1]
        rows = couplings[c * RANK : (c + 1) * RANK, :].astype(f32)
        masked[c * RANK : (c + 1) * RANK, :] = (rows * weights).astype(bf16)


NEAR_CHUNK = 256


def near_windows(traces, recv_a, recv_b, window):
    _, odd = position()
    window[1] = traces[...]
    for recv, right in sides_of(odd, recv_a, recv_b):
        window[jnp.where(right, 2, 0)] = recv[...]
    left, own, right = window[0], window[1], window[2]
    return (
        jnp.concatenate([left, own, right[:, :CLUSTER]], axis=1),
        jnp.concatenate([left[:, CLUSTER:], own, right], axis=1),
    )


def near_1_kernel(traces, recv_a, recv_b, tiles, out, window):
    wide = near_windows(traces, recv_a, recv_b, window)
    for c in range(2):
        out[:, c * CLUSTER : (c + 1) * CLUSTER] = dot(wide[c], tiles[c], NT)


def near_2_kernel(traces, recv_a, recv_b, tiles_hbm, out, window, tiles, sems):
    chunks = [
        pltpu.make_async_copy(
            tiles_hbm.at[i // 2, pl.ds((i % 2) * NEAR_CHUNK, NEAR_CHUNK), :],
            tiles.at[i],
            sems.at[i],
        )
        for i in range(4)
    ]
    for chunk in chunks:
        chunk.start()
    wide = near_windows(traces, recv_a, recv_b, window)
    for i, chunk in enumerate(chunks):
        chunk.wait()
        out[:, i * NEAR_CHUNK : (i + 1) * NEAR_CHUNK] = dot(wide[i // 2], tiles[i], NT)


def far_part(gathered, masked, row_basis, nearby, out):
    g = gathered[...]
    turned = jnp.concatenate([g[:, :, COLS:], g[:, :, :COLS]], axis=2)
    g = jnp.concatenate([g, turned], axis=1).reshape(NDEV * 2 * RANK, NZ)
    coupled = dot(masked[...], g, NN)
    coupled = jnp.transpose(coupled)[:COLS].astype(bf16)
    for c in range(2):
        cut = slice(c * CLUSTER, (c + 1) * CLUSTER)
        part = dot(coupled[:, c * RANK : (c + 1) * RANK], row_basis[c], NN)
        out[:, cut] = nearby[:, cut] + part


def far_1_kernel(
    gathered, masked, row_basis, nearby, order, res_hbm,
    res, placed, send_a, send_b,
    onehot, total, sem,
):
    _, odd = position()
    load = pltpu.make_async_copy(res_hbm, res, sem)
    load.start()
    far_part(gathered, masked, row_basis, nearby, total)
    build_onehot(order, onehot)
    cells = place(total[...], onehot)
    for x in range(XL):
        placed[x] = cells[:, x * NZ : (x + 1) * NZ]
    for send, right in ((send_a, odd == 0), (send_b, odd != 0)):
        for h in (1, 2, 3):
            send[h - 1] = placed[jnp.where(right, XL - h, h - 1)].astype(bf16)
    load.wait()


def far_2_kernel(gathered, masked, row_basis, nearby, out):
    far_part(gathered, masked, row_basis, nearby, out)


class Hbm:
    def __init__(self, value):
        self.value = value


def call(kernel, outs, scratch, *operands, aliases={}):
    vmem = pl.BlockSpec(memory_space=pltpu.VMEM)
    hbm = pl.BlockSpec(memory_space=pltpu.HBM)
    given = [
        pltpu.with_memory_space_constraint(x.value, pltpu.HBM)
        if isinstance(x, Hbm)
        else pltpu.with_memory_space_constraint(x, pltpu.VMEM)
        for x in operands
    ]
    return pl.pallas_call(
        kernel,
        out_shape=[
            pltpu.HBM(x.value.shape, x.value.dtype)
            if isinstance(x, Hbm)
            else pltpu.VMEM(x.shape, x.dtype)
            for x in outs
        ],
        in_specs=[hbm if isinstance(x, Hbm) else vmem for x in operands],
        out_specs=[hbm if isinstance(x, Hbm) else vmem for x in outs],
        scratch_shapes=scratch,
        input_output_aliases=aliases,
        compiler_params=pltpu.CompilerParams(vmem_limit_bytes=24 << 20),
    )(*given)


struct = jax.ShapeDtypeStruct
FIELD = struct((XL, NY, COLS, NZ), f32)
EXT_FIELD = struct((EXT, NY, COLS, NZ), f32)
ONEHOT = pltpu.VMEM((SROW, SROW), bf16)
RAW = pltpu.VMEM((7, XL, NY, NZ), f32)
COEF = struct((6, EXT, NY, NZ), f32)
INV = struct((1, EXT, NY, NZ), f32)
DMA = pltpu.SemaphoreType.DMA


def gather(spread):
    return lax.all_to_all(spread, "dev", split_axis=0, concat_axis=0, tiled=True)


def block_steps(
    field_start, forcing, traction_start, conductivity, reaction, surface_order,
    near_tiles, col_basis, row_basis, couplings, far_leaf,
):
    order = surface_order.reshape(1, SROW)
    wide = NDEV * 2 * RANK
    layer = struct((XL, NY, NZ), f32)
    message = struct((2 * NY + 1, COLS, NZ), bf16)
    far_message = struct((2 * NY, COLS, NZ), bf16)
    values, forcing_near, cond, reac, res, send_a, send_b, far_a, far_b = call(
        first_kernel,
        [FIELD, FIELD, layer, layer, FIELD, message, message, far_message, far_message],
        [
            pltpu.VMEM((1, SROW), jnp.int32), pltpu.VMEM((COLS, SROW), f32), RAW, ONEHOT,
            pltpu.VMEM((XL, COLS, NZ), f32), DMA((4,)), DMA((2, XL)),
        ],
        Hbm(field_start), Hbm(forcing), Hbm(traction_start), Hbm(order),
        Hbm(conductivity), Hbm(reaction),
    )
    recv_a, recv_b = swap(send_a, send_b)
    far_a, far_b = swap(far_a, far_b)
    (masked,) = call(
        mask_kernel,
        [struct((2 * RANK, wide), bf16)],
        [],
        couplings.reshape(2 * RANK, wide), far_leaf,
    )
    message = struct((4 * NY, COLS, NZ), bf16)
    spread_shape = struct((NDEV, RANK, NZ), bf16)
    traces_shape = struct((COLS, SROW), bf16)
    near_shape = struct((COLS, SROW), f32)
    window = pltpu.VMEM((3, COLS, SROW), bf16)
    steps = [EXT_FIELD, EXT_FIELD, EXT_FIELD, FIELD]
    cond_ext, reac_ext, coef, inv, *state = call(
        sweep_1a_kernel,
        [struct((XL + 8, NY, NZ), f32), struct((EXT, NY, NZ), f32), COEF, INV] + steps,
        [],
        values, cond, reac, res, recv_a, recv_b,
    )
    field, res, traces, send_a, send_b, spread, *_ = call(
        sweep_1b_kernel,
        [Hbm(FIELD), Hbm(FIELD), traces_shape, message, message, spread_shape] + steps,
        [RAW, ONEHOT, DMA((2,))],
        values, forcing_near, cond, reac, far_a, far_b, coef, inv, order, col_basis, *state,
        aliases={10 + i: 6 + i for i in range(4)},
    )
    near_a, near_b = swap(traces, traces)
    gathered = gather(spread)
    recv_a, recv_b = swap(send_a, send_b)
    (nearby,) = call(
        near_1_kernel, [near_shape], [window], traces, near_a, near_b, near_tiles
    )
    tract = struct((3, COLS, NZ), bf16)
    res, placed, tract_a, tract_b = call(
        far_1_kernel,
        [FIELD, struct((XL, COLS, NZ), f32), tract, tract],
        [ONEHOT, pltpu.VMEM((COLS, SROW), f32), DMA],
        gathered, masked, row_basis, nearby, order, Hbm(res),
    )
    tract_a, tract_b = swap(tract_a, tract_b)
    values, coef, inv, *state = call(
        sweep_2a_kernel,
        [FIELD, COEF, INV] + steps,
        [DMA((3,))],
        Hbm(field), res, cond_ext, reac_ext, recv_a, recv_b, placed,
    )
    field, traces, spread, *_ = call(
        sweep_2b_kernel,
        [Hbm(FIELD), traces_shape, spread_shape] + steps,
        [ONEHOT, DMA],
        values, recv_a, recv_b, tract_a, tract_b, coef, inv, order, col_basis, *state,
        aliases={9 + i: 3 + i for i in range(4)},
    )
    near_a, near_b = swap(traces, traces)
    gathered = gather(spread)
    (nearby,) = call(
        near_2_kernel,
        [near_shape],
        [window, pltpu.VMEM((4, NEAR_CHUNK, 5 * CLUSTER), bf16), DMA((4,))],
        traces, near_a, near_b, Hbm(near_tiles),
    )
    (traction,) = call(
        far_2_kernel,
        [struct((COLS, SROW), f32)],
        [],
        gathered, masked, row_basis, nearby,
    )
    return field, traction


def solution(mesh):
    in_specs = (
        P("dev", None, "sec", None),
        P("dev", None, "sec", None),
        P("sec", "dev"),
        P("dev", None, None),
        P("dev", None, None),
        P("dev"),
        P("dev", None, None),
        P("dev", None, None),
        P("dev", None, None),
        P("dev", None, None),
        P("dev", None),
    )
    out_specs = (P("dev", None, "sec", None), P("sec", "dev"))
    return jax.shard_map(
        block_steps, mesh=mesh, in_specs=in_specs, out_specs=out_specs, check_vma=False
    )
```

```python
import jax
import jax.numpy as jnp
from jax import lax
from jax.experimental import pallas as pl
from jax.experimental.pallas import tpu as pltpu
from jax.sharding import PartitionSpec as P


CLUSTER = 512
RANK = 32
NDEV = 64
XL = 8
NY = 8
COLS = 64
NZ = 128
SROW = XL * NZ
EXT = XL + 6

f32 = jnp.float32
bf16 = jnp.bfloat16

WEST, EAST, SOUTH, NORTH, LOWER, UPPER = range(6)
NT = (((1,), (1,)), ((), ()))
NN = (((1,), (0,)), ((), ()))


def chebyshev_factors():
    delta = 0.95
    rho = delta
    factors = []
    for _ in range(3):
        following = 1.0 / (2.0 / delta - rho)
        factors.append((following * rho, 2.0 * following / delta))
        rho = following
    return factors


SWAP_A = [(i, i ^ 1) for i in range(NDEV)]
SWAP_B = [(i, i + 1) for i in range(1, NDEV - 1, 2)] + [(i + 1, i) for i in range(1, NDEV - 1, 2)]


def swap(a, b):
    a = lax.ppermute(a, "dev", SWAP_A)
    b = lax.ppermute(b, "dev", SWAP_B)
    return a, b


def dot(a, b, dims):
    return lax.dot_general(a, b, dims, preferred_element_type=f32)


def faces(c, west, east, reaction):
    iy = lax.broadcasted_iota(jnp.int32, (NY, NZ), 0)
    iz = lax.broadcasted_iota(jnp.int32, (NY, NZ), 1)
    south = jnp.where(iy == 0, 0.0, pltpu.roll(c, 1, 0))
    north = pltpu.roll(c, NY - 1, 0)
    lower = jnp.where(iz == 0, 0.0, pltpu.roll(c, 1, 1))
    upper = jnp.where(iz == NZ - 1, 0.0, pltpu.roll(c, NZ - 1, 1))
    fw = 0.5 * (c + west)
    fe = 0.5 * (c + east)
    fs = 0.5 * (c + south)
    fn = jnp.where(iy == NY - 1, 0.0, 0.5 * (c + north))
    fl = 0.5 * (c + lower)
    fu = 0.5 * (c + upper)
    rest = fs + fn + fl + fu + reaction
    fl = jnp.where(iz == 0, 0.0, fl)
    fu = jnp.where(iz == NZ - 1, 0.0, fu)
    return (fw, fe, fs, fn, fl, fu), rest


def row(coef, kind, e, y):
    return coef[kind, e, y : y + 1, :]


def tile(values, e, y):
    return values[e, y].reshape(COLS // 8, 8, NZ)


def put(out, e, y, value):
    out[e, y] = value.reshape(COLS, NZ)


def neighbours(values, west, here, east, coef, e, y):
    v = tile(values, here, y)
    acc = row(coef, WEST, e, y) * tile(values, west, y)
    acc = acc + row(coef, EAST, e, y) * tile(values, east, y)
    acc = acc + row(coef, LOWER, e, y) * pltpu.roll(v, 1, 2)
    acc = acc + row(coef, UPPER, e, y) * pltpu.roll(v, NZ - 1, 2)
    if y > 0:
        acc = acc + row(coef, SOUTH, e, y) * tile(values, here, y - 1)
    if y < NY - 1:
        acc = acc + row(coef, NORTH, e, y) * tile(values, here, y + 1)
    return v, acc


def build_onehot(order, onehot):
    wanted = order[...]
    line = wanted // NZ
    inner = wanted - line * NZ
    cell = lax.broadcasted_iota(jnp.int32, (NZ, SROW), 0).astype(f32).astype(bf16)
    one = jnp.ones((NZ, SROW), bf16)
    for x in range(XL):
        here = jnp.where(line == x, inner, -1).astype(f32).astype(bf16)
        onehot[x * NZ : (x + 1) * NZ, :] = jnp.where(
            cell == jnp.broadcast_to(here, (NZ, SROW)), one, jnp.zeros_like(one)
        )


def place(traction, onehot):
    high = traction.astype(bf16)
    low = (traction - high.astype(f32)).astype(bf16)
    both = dot(jnp.concatenate([high, low], axis=0), onehot[...], NT)
    return both[:COLS] + both[COLS:]


def raw_faces(cond, reac, raw):
    def layer(x, carry):
        sides, rest = faces(
            cond[x], cond[jnp.maximum(x - 1, 0)], cond[jnp.minimum(x + 1, XL - 1)], reac[x]
        )
        sides = list(sides)
        sides[WEST] = jnp.where(x == 0, 0.0, sides[WEST])
        sides[EAST] = jnp.where(x == XL - 1, 0.0, sides[EAST])
        for kind in range(6):
            raw[kind, x] = sides[kind]
        raw[6, x] = rest + sides[WEST] + sides[EAST]
        return carry

    lax.fori_loop(0, XL, layer, 0, unroll=8)


def residual_layer(x, values, forcing, raw, out, placed):
    west = jnp.maximum(x - 1, 0)
    east = jnp.minimum(x + 1, XL - 1)
    for y in range(NY):
        v, acc = neighbours(values, west, x, east, raw, x, y)
        res = tile(forcing, x, y) + acc - row(raw, 6, x, y) * v
        if placed is not None and y == NY - 1:
            res = res + placed[x].reshape(COLS // 8, 8, NZ)
        put(out, x, y, res)


def pack(odd, values, res, sends_near, sends_far, base):
    for near, far, right in zip(sends_near, sends_far, (odd == 0, odd != 0)):

        def source(h):
            return jnp.where(right, XL - h, h - 1)

        def copy(y, carry):
            near[y] = values[source(1), y].astype(bf16)
            near[NY + y] = res[source(1), y].astype(bf16)
            for h in (2, 3):
                far[base + (h - 2) * NY + y] = res[source(h), y].astype(bf16)
            return carry

        lax.fori_loop(0, NY, copy, 0, unroll=2)


def pack_coefficients(odd, cond, reac, send_a, send_b):
    for send, right in ((send_a, odd == 0), (send_b, odd != 0)):

        def source(h):
            return jnp.where(right, XL - h, h - 1)

        rows = [cond[source(h)] for h in (1, 2, 3, 4)] + [reac[source(h)] for h in (1, 2, 3)]
        rows.append(jnp.zeros_like(rows[0]))
        send[2 * NY] = jnp.concatenate(rows, axis=0).astype(bf16)


def position():
    index = lax.axis_index("dev")
    return index, lax.rem(index, 2)


def first_kernel(
    values_hbm, forcing_hbm, traction_hbm, order_hbm, cond_hbm, reac_hbm,
    values, forcing, cond, reac, onehot, res, send_a, send_b, far_a, far_b,
    order, traction, raw, placed, small_sems, sems,
):
    _, odd = position()
    small = [
        pltpu.make_async_copy(source, target, small_sems.at[i])
        for i, (source, target) in enumerate(
            ((order_hbm, order), (traction_hbm, traction), (cond_hbm, cond), (reac_hbm, reac))
        )
    ]
    for copy in small:
        copy.start()

    def layer_copies(x):
        return (
            pltpu.make_async_copy(values_hbm.at[x], values.at[x], sems.at[0, x]),
            pltpu.make_async_copy(forcing_hbm.at[x], forcing.at[x], sems.at[1, x]),
        )

    for x in range(XL):
        for copy in layer_copies(x):
            copy.start()
    small[0].wait()
    build_onehot(order, onehot)
    small[1].wait()
    cells = place(traction[...], onehot)
    for x in range(XL):
        placed[x] = cells[:, x * NZ : (x + 1) * NZ]
    small[2].wait()
    small[3].wait()
    raw_faces(cond, reac, raw)
    pack_coefficients(odd, cond, reac, send_a, send_b)
    for copy in layer_copies(0):
        copy.wait()

    def layer(x, carry):
        @pl.when(x < XL - 1)
        def _():
            for copy in layer_copies(x + 1):
                copy.wait()

        residual_layer(x, values, forcing, raw, res, placed)
        return carry

    lax.fori_loop(0, XL, layer, 0)
    pack(odd, values, res, (send_a, send_b), (far_a, far_b), 0)


def sides_of(odd, recv_a, recv_b):
    return ((recv_a, odd == 0), (recv_b, odd != 0))


def extend(odd, recv_a, recv_b, cond, reac, cond_ext, reac_ext):
    for x in range(XL):
        cond_ext[x + 4] = cond[x]
        reac_ext[x + 3] = reac[x]
    for recv, right in sides_of(odd, recv_a, recv_b):
        rows = recv[2 * NY].astype(f32)
        for h in (1, 2, 3, 4):
            cond_ext[jnp.where(right, 11 + h, 4 - h)] = rows[(h - 1) * NY : h * NY]
        for h in (1, 2, 3):
            reac_ext[jnp.where(right, 10 + h, 3 - h)] = rows[(h + 3) * NY : (h + 4) * NY]


def normalise(index, cond_ext, reac_ext, coef, inv):

    def layer(e, carry):
        sides, rest = faces(cond_ext[e + 1], cond_ext[e], cond_ext[e + 2], reac_ext[e])
        diagonal = rest + sides[WEST] + sides[EAST]
        scale = 1.0 / jnp.where(diagonal > 0.0, diagonal, 1.0)
        outside = ((index == 0) & (e < 3)) | ((index == NDEV - 1) & (e >= XL + 3))
        scale = jnp.where(outside, 0.0, scale)
        for kind in range(6):
            coef[kind, e] = sides[kind] * scale
        inv[0, e] = scale
        return carry

    lax.fori_loop(0, EXT, layer, 0, unroll=7)


def widen(value):
    return value.astype(f32).reshape(COLS // 8, 8, NZ)


def start_own(res, inv, first, placed):
    def own(x, carry):
        for y in range(NY):
            r = tile(res, x, y)
            if placed is not None and y == NY - 1:
                r = r + placed[x].reshape(COLS // 8, 8, NZ)
            put(first, x + 3, y, r * row(inv, 0, x + 3, y))
        return carry

    lax.fori_loop(0, XL, own, 0, unroll=2)


def start_edges(odd, values, recv_a, recv_b, coef, first):
    for recv, right in sides_of(odd, recv_a, recv_b):
        edge = jnp.where(right, XL - 1, 0)
        toward = jnp.where(right, EAST, WEST)
        e = edge + 3
        for y in range(NY):
            gap = widen(recv[y]) - tile(values, edge, y)
            put(first, e, y, tile(first, e, y) + row(coef, toward, e, y) * gap)


def start_halo(h, odd, values, recvs, far, coef, inv, first, tracts):
    messages, base = far
    for side, right in enumerate((odd == 0, odd != 0)):
        edge = jnp.where(right, XL - 1, 0)
        back = jnp.where(right, WEST, EAST)
        e = jnp.where(right, XL + 2 + h, 3 - h)
        for y in range(NY):
            if h == 1:
                r = widen(recvs[side][NY + y])
            else:
                r = widen(messages[side][base + (h - 2) * NY + y])
            if tracts is not None and y == NY - 1:
                r = r + widen(tracts[side][h - 1])
            s = r * row(inv, 0, e, y)
            if h == 1:
                gap = widen(recvs[side][y]) - tile(values, edge, y)
                s = s - row(coef, back, e, y) * gap
            put(first, e, y, s)


def sweeps(done, known, values, coef, first, second, third, out, loads=(), stores=None):
    (a1, b1), (a2, b2), (a3, b3) = chebyshev_factors()

    def step_2(e):
        for y in range(NY):
            v, acc = neighbours(first, e - 1, e, e + 1, coef, e, y)
            put(second, e, y, ((1.0 + a1) / b1) * v + acc)

    def step_3(e):
        for y in range(NY):
            v, acc = neighbours(second, e - 1, e, e + 1, coef, e, y)
            s = tile(first, e, y)
            put(third, e, y, ((1.0 + a2 - b2) / b2) * v + ((b2 - a2) / (b1 * b2)) * s + acc)

    def step_4(e):
        for y in range(NY):
            v, acc = neighbours(third, e - 1, e, e + 1, coef, e, y)
            d = ((1.0 + a3 - b3) / b3) * v - (a3 / (b2 * b3)) * tile(second, e, y) + acc
            d = (b1 * b2 * b3) * d + b3 * tile(first, e, y)
            put(out, e - 3, y, tile(values, e - 3, y) + d)

    middle = EXT // 2
    for level, step in ((1, step_2), (2, step_3), (3, step_4)):
        low = 3 + level - known
        skip = middle if done is None else min(3 + level - done, middle)
        left = skip - low
        if level == 3:
            for load in loads:
                load.wait()
            if stores is not None:
                for e in range(skip, EXT - skip):
                    stores(e - 3).start()
        if left <= 0:
            continue

        def layer(i, carry):
            e = jnp.where(i < left, low + i, EXT - skip + i - left)
            step(e)
            if level == 3 and stores is not None:
                stores(e - 3).start()
            return carry

        lax.fori_loop(0, 2 * left, layer, 0, unroll=2)


def surface(out, col_basis, onehot, traces, spread):
    top = jnp.concatenate([out[x, NY - 1] for x in range(XL)], axis=1).astype(bf16)
    tr = dot(top, onehot[...], NN).astype(bf16)
    traces[...] = tr
    parts = [
        dot(col_basis[c], tr[:, c * CLUSTER : (c + 1) * CLUSTER], NT) for c in range(2)
    ]
    packed = jnp.concatenate(parts, axis=1).astype(bf16)

    def copy(i, carry):
        spread[i] = packed
        return carry

    lax.fori_loop(0, NDEV, copy, 0, unroll=8)


def sweep_1a_kernel(
    values, cond, reac, res, recv_a, recv_b,
    cond_ext, reac_ext, coef, inv, first, second, third, out,
):
    index, odd = position()
    extend(odd, recv_a, recv_b, cond, reac, cond_ext, reac_ext)
    normalise(index, cond_ext, reac_ext, coef, inv)
    start_own(res, inv, first, None)
    start_edges(odd, values, recv_a, recv_b, coef, first)
    start_halo(1, odd, values, (recv_a, recv_b), (None, 0), coef, inv, first, None)
    sweeps(None, 1, values, coef, first, second, third, out)


def sweep_1b_kernel(
    values, forcing, cond, reac, far_a, far_b, coef, inv, onehot, col_basis,
    first_in, second_in, third_in, out_in,
    out_hbm, res_hbm, traces, send_a, send_b, spread, first, second, third, out,
    raw, sems,
):
    _, odd = position()
    for h in (2, 3):
        start_halo(h, odd, values, None, ((far_a, far_b), 0), coef, inv, first, None)

    def out_copy(x):
        return pltpu.make_async_copy(out.at[x], out_hbm.at[x], sems.at[x])

    sweeps(1, 3, values, coef, first, second, third, out, stores=out_copy)
    surface(out, col_basis, onehot, traces, spread)
    raw_faces(cond, reac, raw)

    def layer(x, carry):
        residual_layer(x, out, forcing, raw, second, None)
        return carry

    lax.fori_loop(0, XL, layer, 0, unroll=2)
    res_copy = pltpu.make_async_copy(second.at[pl.ds(0, XL)], res_hbm, sems.at[XL])
    res_copy.start()
    pack(odd, out, second, (send_a, send_b), (send_a, send_b), 2 * NY)
    for x in range(XL):
        out_copy(x).wait()
    res_copy.wait()


def sweep_2a_kernel(
    res, cond_ext, reac_ext, placed,
    coef, inv, first, second, third,
):
    index, _ = position()
    normalise(index, cond_ext, reac_ext, coef, inv)
    start_own(res, inv, first, placed)
    sweeps(None, -1, None, coef, first, second, third, None)


def sweep_2b_kernel(
    values_hbm, recv_a, recv_b, coef, first_in, second_in, third_in,
    values, first, second, third, out,
    sems,
):
    _, odd = position()
    edges = [
        pltpu.make_async_copy(values_hbm.at[x], values.at[x], sems.at[i])
        for i, x in enumerate((0, XL - 1))
    ]
    inner = pl.ds(1, XL - 2)
    inner = pltpu.make_async_copy(values_hbm.at[inner], values.at[inner], sems.at[2])
    for load in edges + [inner]:
        load.start()
    for load in edges:
        load.wait()
    start_edges(odd, values, recv_a, recv_b, coef, first)
    sweeps(-1, 0, values, coef, first, second, third, out, loads=[inner])


def sweep_2c_kernel(
    values, recv_a, recv_b, tract_a, tract_b, coef, inv, onehot, col_basis,
    first_in, second_in, third_in, out_in,
    out_hbm, traces, spread, first, second, third, out,
    sems,
):
    _, odd = position()
    recvs = (recv_a, recv_b)
    for h in (1, 2, 3):
        start_halo(
            h, odd, values, recvs, (recvs, 2 * NY), coef, inv, first, (tract_a, tract_b)
        )

    def out_copy(x):
        return pltpu.make_async_copy(out.at[x], out_hbm.at[x], sems.at[x])

    sweeps(0, 3, values, coef, first, second, third, out, stores=out_copy)
    surface(out, col_basis, onehot, traces, spread)
    for x in range(XL):
        out_copy(x).wait()


def mask_kernel(couplings, leaf, masked):
    wide = NDEV * 2 * RANK
    cluster = lax.broadcasted_iota(jnp.int32, (NDEV * 2, wide), 0)
    lane = lax.broadcasted_iota(jnp.int32, (NDEV * 2, wide), 1)
    spread = jnp.where(lane // RANK == cluster, 1.0, 0.0).astype(bf16)
    for c in range(2):
        flags = jnp.broadcast_to(leaf[c : c + 1, :].astype(f32), (16, NDEV * 2)).astype(bf16)
        weights = dot(flags, spread, NN)[0:1]
        rows = couplings[c * RANK : (c + 1) * RANK, :].astype(f32)
        masked[c * RANK : (c + 1) * RANK, :] = (rows * weights).astype(bf16)


NEAR_CHUNK = 256


def near_windows(traces, recv_a, recv_b, window):
    _, odd = position()
    window[1] = traces[...]
    for recv, right in sides_of(odd, recv_a, recv_b):
        window[jnp.where(right, 2, 0)] = recv[...]
    left, own, right = window[0], window[1], window[2]
    return (
        jnp.concatenate([left, own, right[:, :CLUSTER]], axis=1),
        jnp.concatenate([left[:, CLUSTER:], own, right], axis=1),
    )


def near_1_kernel(traces, recv_a, recv_b, tiles, out, window):
    wide = near_windows(traces, recv_a, recv_b, window)
    for c in range(2):
        out[:, c * CLUSTER : (c + 1) * CLUSTER] = dot(wide[c], tiles[c], NT)


def near_2_kernel(traces, recv_a, recv_b, tiles_hbm, out, window, tiles, sems):
    chunks = [
        pltpu.make_async_copy(
            tiles_hbm.at[i // 2, pl.ds((i % 2) * NEAR_CHUNK, NEAR_CHUNK), :],
            tiles.at[i],
            sems.at[i],
        )
        for i in range(4)
    ]
    for chunk in chunks:
        chunk.start()
    wide = near_windows(traces, recv_a, recv_b, window)
    for i, chunk in enumerate(chunks):
        chunk.wait()
        out[:, i * NEAR_CHUNK : (i + 1) * NEAR_CHUNK] = dot(wide[i // 2], tiles[i], NT)


def far_part(gathered, masked, row_basis, nearby, out):
    g = gathered[...]
    turned = jnp.concatenate([g[:, :, COLS:], g[:, :, :COLS]], axis=2)
    g = jnp.concatenate([g, turned], axis=1).reshape(NDEV * 2 * RANK, NZ)
    coupled = dot(masked[...], g, NN)
    coupled = jnp.transpose(coupled)[:COLS].astype(bf16)
    for c in range(2):
        cut = slice(c * CLUSTER, (c + 1) * CLUSTER)
        part = dot(coupled[:, c * RANK : (c + 1) * RANK], row_basis[c], NN)
        out[:, cut] = nearby[:, cut] + part


def far_1_kernel(
    gathered, masked, row_basis, nearby, order, res_hbm,
    res, onehot, placed, send_a, send_b,
    total, sem,
):
    _, odd = position()
    load = pltpu.make_async_copy(res_hbm, res, sem)
    load.start()
    far_part(gathered, masked, row_basis, nearby, total)
    build_onehot(order, onehot)
    cells = place(total[...], onehot)
    for x in range(XL):
        placed[x] = cells[:, x * NZ : (x + 1) * NZ]
    for send, right in ((send_a, odd == 0), (send_b, odd != 0)):
        for h in (1, 2, 3):
            send[h - 1] = placed[jnp.where(right, XL - h, h - 1)].astype(bf16)
    load.wait()


def far_2_kernel(gathered, masked, row_basis, nearby, out_hbm, out, sem):
    far_part(gathered, masked, row_basis, nearby, out)
    copy = pltpu.make_async_copy(out, out_hbm, sem)
    copy.start()
    copy.wait()


class Hbm:
    def __init__(self, value):
        self.value = value


def call(kernel, outs, scratch, *operands, aliases={}, cost=None):
    vmem = pl.BlockSpec(memory_space=pltpu.VMEM)
    hbm = pl.BlockSpec(memory_space=pltpu.HBM)
    given = [
        pltpu.with_memory_space_constraint(x.value, pltpu.HBM)
        if isinstance(x, Hbm)
        else pltpu.with_memory_space_constraint(x, pltpu.VMEM)
        for x in operands
    ]
    return pl.pallas_call(
        kernel,
        out_shape=[
            pltpu.HBM(x.value.shape, x.value.dtype)
            if isinstance(x, Hbm)
            else pltpu.VMEM(x.shape, x.dtype)
            for x in outs
        ],
        in_specs=[hbm if isinstance(x, Hbm) else vmem for x in operands],
        out_specs=[hbm if isinstance(x, Hbm) else vmem for x in outs],
        scratch_shapes=scratch,
        input_output_aliases=aliases,
        cost_estimate=cost,
        compiler_params=pltpu.CompilerParams(vmem_limit_bytes=24 << 20),
    )(*given)


struct = jax.ShapeDtypeStruct
FIELD = struct((XL, NY, COLS, NZ), f32)
EXT_FIELD = struct((EXT, NY, COLS, NZ), f32)
ONEHOT = struct((SROW, SROW), bf16)
RAW = pltpu.VMEM((7, XL, NY, NZ), f32)
COEF = struct((6, EXT, NY, NZ), f32)
INV = struct((1, EXT, NY, NZ), f32)
DMA = pltpu.SemaphoreType.DMA


def gather(spread):
    return lax.all_to_all(spread, "dev", split_axis=0, concat_axis=0, tiled=True)


def block_steps(
    field_start, forcing, traction_start, conductivity, reaction, surface_order,
    near_tiles, col_basis, row_basis, couplings, far_leaf,
):
    order = surface_order.reshape(1, SROW)
    wide = NDEV * 2 * RANK
    layer = struct((XL, NY, NZ), f32)
    message = struct((2 * NY + 1, COLS, NZ), bf16)
    far_message = struct((2 * NY, COLS, NZ), bf16)
    values, forcing_near, cond, reac, onehot, res, send_a, send_b, far_a, far_b = call(
        first_kernel,
        [FIELD, FIELD, layer, layer, ONEHOT, FIELD, message, message, far_message, far_message],
        [
            pltpu.VMEM((1, SROW), jnp.int32), pltpu.VMEM((COLS, SROW), f32), RAW,
            pltpu.VMEM((XL, COLS, NZ), f32), DMA((4,)), DMA((2, XL)),
        ],
        Hbm(field_start), Hbm(forcing), Hbm(traction_start), Hbm(order),
        Hbm(conductivity), Hbm(reaction),
    )
    recv_a, recv_b = swap(send_a, send_b)
    far_a, far_b = swap(far_a, far_b)
    (masked,) = call(
        mask_kernel,
        [struct((2 * RANK, wide), bf16)],
        [],
        couplings.reshape(2 * RANK, wide), far_leaf,
    )
    message = struct((4 * NY, COLS, NZ), bf16)
    spread_shape = struct((NDEV, RANK, NZ), bf16)
    traces_shape = struct((COLS, SROW), bf16)
    near_shape = struct((COLS, SROW), f32)
    window = pltpu.VMEM((3, COLS, SROW), bf16)
    steps = [EXT_FIELD, EXT_FIELD, EXT_FIELD, FIELD]
    cond_ext, reac_ext, coef, inv, *state = call(
        sweep_1a_kernel,
        [struct((XL + 8, NY, NZ), f32), struct((EXT, NY, NZ), f32), COEF, INV] + steps,
        [],
        values, cond, reac, res, recv_a, recv_b,
    )
    field, res, traces, send_a, send_b, spread, *_ = call(
        sweep_1b_kernel,
        [Hbm(FIELD), Hbm(FIELD), traces_shape, message, message, spread_shape] + steps,
        [RAW, DMA((XL + 1,))],
        values, forcing_near, cond, reac, far_a, far_b, coef, inv, onehot, col_basis, *state,
        aliases={10 + i: 6 + i for i in range(4)},
    )
    near_a, near_b = swap(traces, traces)
    gathered = gather(spread)
    recv_a, recv_b = swap(send_a, send_b)
    (nearby,) = call(
        near_1_kernel, [near_shape], [window], traces, near_a, near_b, near_tiles
    )
    tract = struct((3, COLS, NZ), bf16)
    res, onehot, placed, tract_a, tract_b = call(
        far_1_kernel,
        [FIELD, ONEHOT, struct((XL, COLS, NZ), f32), tract, tract],
        [pltpu.VMEM((COLS, SROW), f32), DMA],
        gathered, masked, row_basis, nearby, order, Hbm(res),
    )
    tract_a, tract_b = swap(tract_a, tract_b)
    coef, inv, *state = call(
        sweep_2a_kernel,
        [COEF, INV, EXT_FIELD, EXT_FIELD, EXT_FIELD],
        [],
        res, cond_ext, reac_ext, placed,
    )
    values, *state = call(
        sweep_2b_kernel,
        [FIELD] + steps,
        [DMA((3,))],
        Hbm(field), recv_a, recv_b, coef, *state,
        aliases={4 + i: 1 + i for i in range(3)},
    )
    field, traces, spread, *_ = call(
        sweep_2c_kernel,
        [Hbm(FIELD), traces_shape, spread_shape] + steps,
        [DMA((XL,))],
        values, recv_a, recv_b, tract_a, tract_b, coef, inv, onehot, col_basis, *state,
        aliases={9 + i: 3 + i for i in range(4)},
    )
    near_a, near_b = swap(traces, traces)
    gathered = gather(spread)
    (nearby,) = call(
        near_2_kernel,
        [near_shape],
        [window, pltpu.VMEM((4, NEAR_CHUNK, 5 * CLUSTER), bf16), DMA((4,))],
        traces, near_a, near_b, Hbm(near_tiles),
    )
    (traction,) = call(
        far_2_kernel,
        [Hbm(struct((COLS, SROW), f32))],
        [pltpu.VMEM((COLS, SROW), f32), DMA],
        gathered, masked, row_basis, nearby,
    )
    return field, traction


def solution(mesh):
    in_specs = (
        P("dev", None, "sec", None),
        P("dev", None, "sec", None),
        P("sec", "dev"),
        P("dev", None, None),
        P("dev", None, None),
        P("dev"),
        P("dev", None, None),
        P("dev", None, None),
        P("dev", None, None),
        P("dev", None, None),
        P("dev", None),
    )
    out_specs = (P("dev", None, "sec", None), P("sec", "dev"))
    return jax.shard_map(
        block_steps, mesh=mesh, in_specs=in_specs, out_specs=out_specs, check_vma=False
    )
```

```python
import jax
import jax.numpy as jnp
from jax import lax
from jax.experimental import pallas as pl
from jax.experimental.pallas import tpu as pltpu
from jax.sharding import PartitionSpec as P


CLUSTER = 512
RANK = 32
NDEV = 64
XL = 8
NY = 8
COLS = 64
NZ = 128
SROW = XL * NZ
EXT = XL + 6

f32 = jnp.float32
bf16 = jnp.bfloat16

WEST, EAST, SOUTH, NORTH, LOWER, UPPER = range(6)
NT = (((1,), (1,)), ((), ()))
NN = (((1,), (0,)), ((), ()))


def chebyshev_factors():
    delta = 0.95
    rho = delta
    factors = []
    for _ in range(3):
        following = 1.0 / (2.0 / delta - rho)
        factors.append((following * rho, 2.0 * following / delta))
        rho = following
    return factors


SWAP_A = [(i, i ^ 1) for i in range(NDEV)]
SWAP_B = [(i, i + 1) for i in range(1, NDEV - 1, 2)] + [(i + 1, i) for i in range(1, NDEV - 1, 2)]


def swap(a, b):
    a = lax.ppermute(a, "dev", SWAP_A)
    b = lax.ppermute(b, "dev", SWAP_B)
    return a, b


def dot(a, b, dims):
    return lax.dot_general(a, b, dims, preferred_element_type=f32)


def faces(c, west, east, reaction):
    iy = lax.broadcasted_iota(jnp.int32, (NY, NZ), 0)
    iz = lax.broadcasted_iota(jnp.int32, (NY, NZ), 1)
    south = jnp.where(iy == 0, 0.0, pltpu.roll(c, 1, 0))
    north = pltpu.roll(c, NY - 1, 0)
    lower = jnp.where(iz == 0, 0.0, pltpu.roll(c, 1, 1))
    upper = jnp.where(iz == NZ - 1, 0.0, pltpu.roll(c, NZ - 1, 1))
    fw = 0.5 * (c + west)
    fe = 0.5 * (c + east)
    fs = 0.5 * (c + south)
    fn = jnp.where(iy == NY - 1, 0.0, 0.5 * (c + north))
    fl = 0.5 * (c + lower)
    fu = 0.5 * (c + upper)
    rest = fs + fn + fl + fu + reaction
    fl = jnp.where(iz == 0, 0.0, fl)
    fu = jnp.where(iz == NZ - 1, 0.0, fu)
    return (fw, fe, fs, fn, fl, fu), rest


def row(coef, kind, e, y):
    return coef[kind, e, y : y + 1, :]


def tile(values, e, y):
    return values[e, y].reshape(COLS // 8, 8, NZ)


def put(out, e, y, value):
    out[e, y] = value.reshape(COLS, NZ)


def neighbours(values, west, here, east, coef, e, y):
    v = tile(values, here, y)
    acc = row(coef, WEST, e, y) * tile(values, west, y)
    acc = acc + row(coef, EAST, e, y) * tile(values, east, y)
    acc = acc + row(coef, LOWER, e, y) * pltpu.roll(v, 1, 2)
    acc = acc + row(coef, UPPER, e, y) * pltpu.roll(v, NZ - 1, 2)
    if y > 0:
        acc = acc + row(coef, SOUTH, e, y) * tile(values, here, y - 1)
    if y < NY - 1:
        acc = acc + row(coef, NORTH, e, y) * tile(values, here, y + 1)
    return v, acc


def build_onehot(order, onehot):
    wanted = order[...]
    line = wanted // NZ
    inner = wanted - line * NZ
    cell = lax.broadcasted_iota(jnp.int32, (NZ, SROW), 0).astype(f32).astype(bf16)
    one = jnp.ones((NZ, SROW), bf16)
    for x in range(XL):
        here = jnp.where(line == x, inner, -1).astype(f32).astype(bf16)
        onehot[x * NZ : (x + 1) * NZ, :] = jnp.where(
            cell == jnp.broadcast_to(here, (NZ, SROW)), one, jnp.zeros_like(one)
        )


def place(traction, onehot):
    high = traction.astype(bf16)
    low = (traction - high.astype(f32)).astype(bf16)
    both = dot(jnp.concatenate([high, low], axis=0), onehot[...], NT)
    return both[:COLS] + both[COLS:]


def raw_faces(cond, reac, raw):
    def layer(x, carry):
        sides, rest = faces(
            cond[x], cond[jnp.maximum(x - 1, 0)], cond[jnp.minimum(x + 1, XL - 1)], reac[x]
        )
        sides = list(sides)
        sides[WEST] = jnp.where(x == 0, 0.0, sides[WEST])
        sides[EAST] = jnp.where(x == XL - 1, 0.0, sides[EAST])
        for kind in range(6):
            raw[kind, x] = sides[kind]
        raw[6, x] = rest + sides[WEST] + sides[EAST]
        return carry

    lax.fori_loop(0, XL, layer, 0, unroll=8)


def residual_layer(x, values, forcing, raw, out, placed):
    west = jnp.maximum(x - 1, 0)
    east = jnp.minimum(x + 1, XL - 1)
    for y in range(NY):
        v, acc = neighbours(values, west, x, east, raw, x, y)
        res = tile(forcing, x, y) + acc - row(raw, 6, x, y) * v
        if placed is not None and y == NY - 1:
            res = res + placed[x].reshape(COLS // 8, 8, NZ)
        put(out, x, y, res)


def pack_near(odd, values, res, sends):
    for send, right in zip(sends, (odd == 0, odd != 0)):
        edge = jnp.where(right, XL - 1, 0)

        def copy(y, carry):
            send[y] = values[edge, y].astype(bf16)
            send[NY + y] = res[edge, y].astype(bf16)
            return carry

        lax.fori_loop(0, NY, copy, 0, unroll=2)


def pack_far(odd, res, sends, base):
    for send, right in zip(sends, (odd == 0, odd != 0)):

        def copy(y, carry):
            for h in (2, 3):
                layer = jnp.where(right, XL - h, h - 1)
                send[base + (h - 2) * NY + y] = res[layer, y].astype(bf16)
            return carry

        lax.fori_loop(0, NY, copy, 0, unroll=2)


def pack_coefficients(odd, cond, reac, send_a, send_b):
    for send, right in ((send_a, odd == 0), (send_b, odd != 0)):

        def source(h):
            return jnp.where(right, XL - h, h - 1)

        rows = [cond[source(h)] for h in (1, 2, 3, 4)] + [reac[source(h)] for h in (1, 2, 3)]
        rows.append(jnp.zeros_like(rows[0]))
        send[2 * NY] = jnp.concatenate(rows, axis=0).astype(bf16)


def position():
    index = lax.axis_index("dev")
    return index, lax.rem(index, 2)


def first_a_kernel(
    values_hbm, forcing_hbm, traction_hbm, order_hbm, cond_hbm, reac_hbm,
    values, forcing, cond, reac, onehot, placed, raw, res, send_a, send_b,
    order, traction, small_sems, sems,
):
    _, odd = position()
    small = [
        pltpu.make_async_copy(source, target, small_sems.at[i])
        for i, (source, target) in enumerate(
            ((order_hbm, order), (traction_hbm, traction), (cond_hbm, cond), (reac_hbm, reac))
        )
    ]
    last = XL - 1
    layers = [
        pltpu.make_async_copy(source.at[x], target.at[x], sems.at[i])
        for i, (source, target, x) in enumerate(
            (
                (values_hbm, values, 0), (values_hbm, values, 1), (forcing_hbm, forcing, 0),
                (values_hbm, values, last), (values_hbm, values, last - 1),
                (forcing_hbm, forcing, last),
            )
        )
    ]
    for copy in small + layers:
        copy.start()
    small[0].wait()
    build_onehot(order, onehot)
    small[1].wait()
    cells = place(traction[...], onehot)
    for x in range(XL):
        placed[x] = cells[:, x * NZ : (x + 1) * NZ]
    small[2].wait()
    small[3].wait()
    raw_faces(cond, reac, raw)
    pack_coefficients(odd, cond, reac, send_a, send_b)
    for copy in layers:
        copy.wait()

    def layer(i, carry):
        residual_layer(i * last, values, forcing, raw, res, placed)
        return carry

    lax.fori_loop(0, 2, layer, 0, unroll=2)
    pack_near(odd, values, res, (send_a, send_b))


def first_b_kernel(
    values_hbm, forcing_hbm, placed, raw, values_in, forcing_in, res_in,
    values, forcing, res, far_a, far_b,
    sems,
):
    _, odd = position()

    def values_copy(x):
        return pltpu.make_async_copy(values_hbm.at[x], values.at[x], sems.at[0, x])

    def forcing_copy(x):
        return pltpu.make_async_copy(forcing_hbm.at[x], forcing.at[x], sems.at[1, x])

    for x in range(1, XL - 1):
        if x < XL - 3:
            values_copy(x + 1).start()
        forcing_copy(x).start()

    def layer(x, carry):
        @pl.when(x < XL - 3)
        def _():
            values_copy(x + 1).wait()

        forcing_copy(x).wait()
        residual_layer(x, values, forcing, raw, res, placed)
        return carry

    lax.fori_loop(1, XL - 1, layer, 0)
    pack_far(odd, res, (far_a, far_b), 0)


def sides_of(odd, recv_a, recv_b):
    return ((recv_a, odd == 0), (recv_b, odd != 0))


def extend(odd, recv_a, recv_b, cond, reac, cond_ext, reac_ext):
    for x in range(XL):
        cond_ext[x + 4] = cond[x]
        reac_ext[x + 3] = reac[x]
    for recv, right in sides_of(odd, recv_a, recv_b):
        rows = recv[2 * NY].astype(f32)
        for h in (1, 2, 3, 4):
            cond_ext[jnp.where(right, 11 + h, 4 - h)] = rows[(h - 1) * NY : h * NY]
        for h in (1, 2, 3):
            reac_ext[jnp.where(right, 10 + h, 3 - h)] = rows[(h + 3) * NY : (h + 4) * NY]


def normalise(index, cond_ext, reac_ext, coef, inv):

    def layer(e, carry):
        sides, rest = faces(cond_ext[e + 1], cond_ext[e], cond_ext[e + 2], reac_ext[e])
        diagonal = rest + sides[WEST] + sides[EAST]
        scale = 1.0 / jnp.where(diagonal > 0.0, diagonal, 1.0)
        outside = ((index == 0) & (e < 3)) | ((index == NDEV - 1) & (e >= XL + 3))
        scale = jnp.where(outside, 0.0, scale)
        for kind in range(6):
            coef[kind, e] = sides[kind] * scale
        inv[0, e] = scale
        return carry

    lax.fori_loop(0, EXT, layer, 0, unroll=7)


def widen(value):
    return value.astype(f32).reshape(COLS // 8, 8, NZ)


def start_own(res, inv, first, placed):
    def own(x, carry):
        for y in range(NY):
            r = tile(res, x, y)
            if placed is not None and y == NY - 1:
                r = r + placed[x].reshape(COLS // 8, 8, NZ)
            put(first, x + 3, y, r * row(inv, 0, x + 3, y))
        return carry

    lax.fori_loop(0, XL, own, 0, unroll=2)


def start_edges(odd, values, recv_a, recv_b, coef, first):
    for recv, right in sides_of(odd, recv_a, recv_b):
        edge = jnp.where(right, XL - 1, 0)
        toward = jnp.where(right, EAST, WEST)
        e = edge + 3
        for y in range(NY):
            gap = widen(recv[y]) - tile(values, edge, y)
            put(first, e, y, tile(first, e, y) + row(coef, toward, e, y) * gap)


def start_halo(h, odd, values, recvs, far, coef, inv, first, tracts):
    messages, base = far
    for side, right in enumerate((odd == 0, odd != 0)):
        edge = jnp.where(right, XL - 1, 0)
        back = jnp.where(right, WEST, EAST)
        e = jnp.where(right, XL + 2 + h, 3 - h)
        for y in range(NY):
            if h == 1:
                r = widen(recvs[side][NY + y])
            else:
                r = widen(messages[side][base + (h - 2) * NY + y])
            if tracts is not None and y == NY - 1:
                r = r + widen(tracts[side][h - 1])
            s = r * row(inv, 0, e, y)
            if h == 1:
                gap = widen(recvs[side][y]) - tile(values, edge, y)
                s = s - row(coef, back, e, y) * gap
            put(first, e, y, s)


def sweeps(done, known, values, coef, first, second, third, out, loads=(), stores=None):
    (a1, b1), (a2, b2), (a3, b3) = chebyshev_factors()

    def step_2(e):
        for y in range(NY):
            v, acc = neighbours(first, e - 1, e, e + 1, coef, e, y)
            put(second, e, y, ((1.0 + a1) / b1) * v + acc)

    def step_3(e):
        for y in range(NY):
            v, acc = neighbours(second, e - 1, e, e + 1, coef, e, y)
            s = tile(first, e, y)
            put(third, e, y, ((1.0 + a2 - b2) / b2) * v + ((b2 - a2) / (b1 * b2)) * s + acc)

    def step_4(e):
        for y in range(NY):
            v, acc = neighbours(third, e - 1, e, e + 1, coef, e, y)
            d = ((1.0 + a3 - b3) / b3) * v - (a3 / (b2 * b3)) * tile(second, e, y) + acc
            d = (b1 * b2 * b3) * d + b3 * tile(first, e, y)
            put(out, e - 3, y, tile(values, e - 3, y) + d)

    middle = EXT // 2
    for level, step in ((1, step_2), (2, step_3), (3, step_4)):
        low = 3 + level - known
        skip = middle if done is None else min(3 + level - done, middle)
        left = skip - low
        if level == 3:
            for load in loads:
                load.wait()
            if stores is not None:
                for e in range(skip, EXT - skip):
                    stores(e - 3).start()
        if left <= 0:
            continue

        def layer(i, carry):
            e = jnp.where(i < left, low + i, EXT - skip + i - left)
            step(e)
            if level == 3 and stores is not None:
                stores(e - 3).start()
            return carry

        lax.fori_loop(0, 2 * left, layer, 0, unroll=2)


def surface(out, col_basis, onehot, traces, spread):
    top = jnp.concatenate([out[x, NY - 1] for x in range(XL)], axis=1).astype(bf16)
    tr = dot(top, onehot[...], NN).astype(bf16)
    traces[...] = tr
    parts = [
        dot(col_basis[c], tr[:, c * CLUSTER : (c + 1) * CLUSTER], NT) for c in range(2)
    ]
    packed = jnp.concatenate(parts, axis=1).astype(bf16)

    def copy(i, carry):
        spread[i] = packed
        return carry

    lax.fori_loop(0, NDEV, copy, 0, unroll=8)


def sweep_1a_kernel(
    values, cond, reac, res, recv_a, recv_b,
    cond_ext, reac_ext, coef, inv, first, second, third, out,
):
    index, odd = position()
    extend(odd, recv_a, recv_b, cond, reac, cond_ext, reac_ext)
    normalise(index, cond_ext, reac_ext, coef, inv)
    start_own(res, inv, first, None)
    start_edges(odd, values, recv_a, recv_b, coef, first)
    start_halo(1, odd, values, (recv_a, recv_b), (None, 0), coef, inv, first, None)
    sweeps(None, 1, values, coef, first, second, third, out)


def sweep_1b_kernel(
    values, forcing, raw, far_a, far_b, coef, inv, onehot, col_basis,
    first_in, second_in, third_in, out_in,
    out_hbm, res_hbm, traces, send_a, send_b, spread, first, second, third, out,
    sems,
):
    _, odd = position()
    for h in (2, 3):
        start_halo(h, odd, values, None, ((far_a, far_b), 0), coef, inv, first, None)

    def out_copy(x):
        return pltpu.make_async_copy(out.at[x], out_hbm.at[x], sems.at[x])

    sweeps(1, 3, values, coef, first, second, third, out, stores=out_copy)
    surface(out, col_basis, onehot, traces, spread)

    def layer(x, carry):
        residual_layer(x, out, forcing, raw, second, None)
        return carry

    lax.fori_loop(0, XL, layer, 0, unroll=2)
    res_copy = pltpu.make_async_copy(second.at[pl.ds(0, XL)], res_hbm, sems.at[XL])
    res_copy.start()
    pack_near(odd, out, second, (send_a, send_b))
    pack_far(odd, second, (send_a, send_b), 2 * NY)
    for x in range(XL):
        out_copy(x).wait()
    res_copy.wait()


def sweep_2a_kernel(
    res, cond_ext, reac_ext, placed,
    coef, inv, first, second, third,
):
    index, _ = position()
    normalise(index, cond_ext, reac_ext, coef, inv)
    start_own(res, inv, first, placed)
    sweeps(None, -1, None, coef, first, second, third, None)


def sweep_2b_kernel(
    values_hbm, recv_a, recv_b, coef, first_in, second_in, third_in,
    values, first, second, third, out,
    sems,
):
    _, odd = position()
    edges = [
        pltpu.make_async_copy(values_hbm.at[x], values.at[x], sems.at[i])
        for i, x in enumerate((0, XL - 1))
    ]
    inner = pl.ds(1, XL - 2)
    inner = pltpu.make_async_copy(values_hbm.at[inner], values.at[inner], sems.at[2])
    for load in edges + [inner]:
        load.start()
    for load in edges:
        load.wait()
    start_edges(odd, values, recv_a, recv_b, coef, first)
    sweeps(-1, 0, values, coef, first, second, third, out, loads=[inner])


def sweep_2c_kernel(
    values, recv_a, recv_b, tract_a, tract_b, coef, inv, onehot, col_basis,
    first_in, second_in, third_in, out_in,
    out_hbm, traces, spread, first, second, third, out,
    sems,
):
    _, odd = position()
    recvs = (recv_a, recv_b)
    for h in (1, 2, 3):
        start_halo(
            h, odd, values, recvs, (recvs, 2 * NY), coef, inv, first, (tract_a, tract_b)
        )

    def out_copy(x):
        return pltpu.make_async_copy(out.at[x], out_hbm.at[x], sems.at[x])

    sweeps(0, 3, values, coef, first, second, third, out, stores=out_copy)
    surface(out, col_basis, onehot, traces, spread)
    for x in range(XL):
        out_copy(x).wait()


def mask_kernel(couplings, leaf, masked):
    wide = NDEV * 2 * RANK
    cluster = lax.broadcasted_iota(jnp.int32, (NDEV * 2, wide), 0)
    lane = lax.broadcasted_iota(jnp.int32, (NDEV * 2, wide), 1)
    spread = jnp.where(lane // RANK == cluster, 1.0, 0.0).astype(bf16)
    for c in range(2):
        flags = jnp.broadcast_to(leaf[c : c + 1, :].astype(f32), (16, NDEV * 2)).astype(bf16)
        weights = dot(flags, spread, NN)[0:1]
        rows = couplings[c * RANK : (c + 1) * RANK, :].astype(f32)
        masked[c * RANK : (c + 1) * RANK, :] = (rows * weights).astype(bf16)


def near_windows(traces, recv_a, recv_b, window):
    _, odd = position()
    window[1] = traces[...]
    for recv, right in sides_of(odd, recv_a, recv_b):
        window[jnp.where(right, 2, 0)] = recv[...]
    left, own, right = window[0], window[1], window[2]
    return (
        jnp.concatenate([left, own, right[:, :CLUSTER]], axis=1),
        jnp.concatenate([left[:, CLUSTER:], own, right], axis=1),
    )


def near_1_kernel(traces, recv_a, recv_b, tiles, out, window):
    wide = near_windows(traces, recv_a, recv_b, window)
    for c in range(2):
        out[:, c * CLUSTER : (c + 1) * CLUSTER] = dot(wide[c], tiles[c], NT)


def add_side(side, tiles, out, right):
    if right:
        out[:, :CLUSTER] += dot(side[:, :CLUSTER], tiles[0, :, 4 * CLUSTER :], NT)
        out[:, CLUSTER:] += dot(side[...], tiles[1, :, 3 * CLUSTER :], NT)
    else:
        out[:, :CLUSTER] += dot(side[...], tiles[0, :, : 2 * CLUSTER], NT)
        out[:, CLUSTER:] += dot(side[:, CLUSTER:], tiles[1, :, :CLUSTER], NT)


def near_2a_kernel(traces, recv_a, tiles_hbm, out, tiles, sems):
    _, odd = position()
    half = CLUSTER // 2
    chunks = []
    for i in range(4):
        rows = pl.ds((i % 2) * half, half)
        chunks.append(
            pltpu.make_async_copy(
                tiles_hbm.at[i // 2, rows, :], tiles.at[i // 2, rows, :], sems.at[i]
            )
        )
    for chunk in chunks:
        chunk.start()
    for i, chunk in enumerate(chunks):
        chunk.wait()
        c, k = i // 2, i % 2
        own = tiles[c, k * half : (k + 1) * half, (2 - c) * CLUSTER : (4 - c) * CLUSTER]
        out[:, i * half : (i + 1) * half] = dot(traces[...], own, NT)

    @pl.when(odd == 0)
    def _():
        add_side(recv_a, tiles, out, True)

    @pl.when(odd != 0)
    def _():
        add_side(recv_a, tiles, out, False)


def near_2b_kernel(recv_b, tiles, nearby, out):
    _, odd = position()

    @pl.when(odd == 0)
    def _():
        add_side(recv_b, tiles, out, False)

    @pl.when(odd != 0)
    def _():
        add_side(recv_b, tiles, out, True)


def far_part(gathered, masked, row_basis, nearby, out):
    g = gathered[...]
    turned = jnp.concatenate([g[:, :, COLS:], g[:, :, :COLS]], axis=2)
    g = jnp.concatenate([g, turned], axis=1).reshape(NDEV * 2 * RANK, NZ)
    coupled = dot(masked[...], g, NN)
    coupled = jnp.transpose(coupled)[:COLS].astype(bf16)
    for c in range(2):
        cut = slice(c * CLUSTER, (c + 1) * CLUSTER)
        part = dot(coupled[:, c * RANK : (c + 1) * RANK], row_basis[c], NN)
        out[:, cut] = nearby[:, cut] + part


def far_1_kernel(
    gathered, masked, row_basis, nearby, order, res_hbm,
    res, onehot, placed, send_a, send_b,
    total, sem,
):
    _, odd = position()
    load = pltpu.make_async_copy(res_hbm, res, sem)
    load.start()
    far_part(gathered, masked, row_basis, nearby, total)
    build_onehot(order, onehot)
    cells = place(total[...], onehot)
    for x in range(XL):
        placed[x] = cells[:, x * NZ : (x + 1) * NZ]
    for send, right in ((send_a, odd == 0), (send_b, odd != 0)):
        for h in (1, 2, 3):
            send[h - 1] = placed[jnp.where(right, XL - h, h - 1)].astype(bf16)
    load.wait()


def far_2_kernel(gathered, masked, row_basis, nearby, out_hbm, out, sem):
    far_part(gathered, masked, row_basis, nearby, out)
    copy = pltpu.make_async_copy(out, out_hbm, sem)
    copy.start()
    copy.wait()


class Hbm:
    def __init__(self, value):
        self.value = value


def call(kernel, outs, scratch, *operands, aliases={}, cost=None):
    vmem = pl.BlockSpec(memory_space=pltpu.VMEM)
    hbm = pl.BlockSpec(memory_space=pltpu.HBM)
    given = [
        pltpu.with_memory_space_constraint(x.value, pltpu.HBM)
        if isinstance(x, Hbm)
        else pltpu.with_memory_space_constraint(x, pltpu.VMEM)
        for x in operands
    ]
    return pl.pallas_call(
        kernel,
        out_shape=[
            pltpu.HBM(x.value.shape, x.value.dtype)
            if isinstance(x, Hbm)
            else pltpu.VMEM(x.shape, x.dtype)
            for x in outs
        ],
        in_specs=[hbm if isinstance(x, Hbm) else vmem for x in operands],
        out_specs=[hbm if isinstance(x, Hbm) else vmem for x in outs],
        scratch_shapes=scratch,
        input_output_aliases=aliases,
        cost_estimate=cost,
        compiler_params=pltpu.CompilerParams(vmem_limit_bytes=24 << 20),
    )(*given)


struct = jax.ShapeDtypeStruct
FIELD = struct((XL, NY, COLS, NZ), f32)
EXT_FIELD = struct((EXT, NY, COLS, NZ), f32)
ONEHOT = struct((SROW, SROW), bf16)
RAW = struct((7, XL, NY, NZ), f32)
COEF = struct((6, EXT, NY, NZ), f32)
INV = struct((1, EXT, NY, NZ), f32)
DMA = pltpu.SemaphoreType.DMA


def gather(spread):
    return lax.all_to_all(spread, "dev", split_axis=0, concat_axis=0, tiled=True)


def block_steps(
    field_start, forcing, traction_start, conductivity, reaction, surface_order,
    near_tiles, col_basis, row_basis, couplings, far_leaf,
):
    order = surface_order.reshape(1, SROW)
    wide = NDEV * 2 * RANK
    layer = struct((XL, NY, NZ), f32)
    message = struct((2 * NY + 1, COLS, NZ), bf16)
    far_message = struct((2 * NY, COLS, NZ), bf16)
    placed_shape = struct((XL, COLS, NZ), f32)
    values, forcing_near, cond, reac, onehot, placed, raw, res, send_a, send_b = call(
        first_a_kernel,
        [FIELD, FIELD, layer, layer, ONEHOT, placed_shape, RAW, FIELD, message, message],
        [pltpu.VMEM((1, SROW), jnp.int32), pltpu.VMEM((COLS, SROW), f32), DMA((4,)), DMA((6,))],
        Hbm(field_start), Hbm(forcing), Hbm(traction_start), Hbm(order),
        Hbm(conductivity), Hbm(reaction),
    )
    recv_a, recv_b = swap(send_a, send_b)
    values, forcing_near, res, far_a, far_b = call(
        first_b_kernel,
        [FIELD, FIELD, FIELD, far_message, far_message],
        [DMA((2, XL))],
        Hbm(field_start), Hbm(forcing), placed, raw, values, forcing_near, res,
        aliases={4: 0, 5: 1, 6: 2},
    )
    far_a, far_b = swap(far_a, far_b)
    (masked,) = call(
        mask_kernel,
        [struct((2 * RANK, wide), bf16)],
        [],
        couplings.reshape(2 * RANK, wide), far_leaf,
    )
    message = struct((4 * NY, COLS, NZ), bf16)
    spread_shape = struct((NDEV, RANK, NZ), bf16)
    traces_shape = struct((COLS, SROW), bf16)
    near_shape = struct((COLS, SROW), f32)
    window = pltpu.VMEM((3, COLS, SROW), bf16)
    steps = [EXT_FIELD, EXT_FIELD, EXT_FIELD, FIELD]
    cond_ext, reac_ext, coef, inv, *state = call(
        sweep_1a_kernel,
        [struct((XL + 8, NY, NZ), f32), struct((EXT, NY, NZ), f32), COEF, INV] + steps,
        [],
        values, cond, reac, res, recv_a, recv_b,
    )
    field, res, traces, send_a, send_b, spread, *_ = call(
        sweep_1b_kernel,
        [Hbm(FIELD), Hbm(FIELD), traces_shape, message, message, spread_shape] + steps,
        [DMA((XL + 1,))],
        values, forcing_near, raw, far_a, far_b, coef, inv, onehot, col_basis, *state,
        aliases={9 + i: 6 + i for i in range(4)},
    )
    near_a, near_b = swap(traces, traces)
    gathered = gather(spread)
    recv_a, recv_b = swap(send_a, send_b)
    (nearby,) = call(
        near_1_kernel, [near_shape], [window], traces, near_a, near_b, near_tiles
    )
    tract = struct((3, COLS, NZ), bf16)
    res, onehot, placed, tract_a, tract_b = call(
        far_1_kernel,
        [FIELD, ONEHOT, struct((XL, COLS, NZ), f32), tract, tract],
        [pltpu.VMEM((COLS, SROW), f32), DMA],
        gathered, masked, row_basis, nearby, order, Hbm(res),
    )
    tract_a, tract_b = swap(tract_a, tract_b)
    coef, inv, *state = call(
        sweep_2a_kernel,
        [COEF, INV, EXT_FIELD, EXT_FIELD, EXT_FIELD],
        [],
        res, cond_ext, reac_ext, placed,
    )
    values, *state = call(
        sweep_2b_kernel,
        [FIELD] + steps,
        [DMA((3,))],
        Hbm(field), recv_a, recv_b, coef, *state,
        aliases={4 + i: 1 + i for i in range(3)},
    )
    field, traces, spread, *_ = call(
        sweep_2c_kernel,
        [Hbm(FIELD), traces_shape, spread_shape] + steps,
        [DMA((XL,))],
        values, recv_a, recv_b, tract_a, tract_b, coef, inv, onehot, col_basis, *state,
        aliases={9 + i: 3 + i for i in range(4)},
    )
    near_a, near_b = swap(traces, traces)
    gathered = gather(spread)
    nearby, tiles = call(
        near_2a_kernel,
        [near_shape, struct((2, CLUSTER, 5 * CLUSTER), bf16)],
        [DMA((4,))],
        traces, near_a, Hbm(near_tiles),
    )
    (nearby,) = call(
        near_2b_kernel, [near_shape], [], near_b, tiles, nearby, aliases={2: 0}
    )
    (traction,) = call(
        far_2_kernel,
        [Hbm(struct((COLS, SROW), f32))],
        [pltpu.VMEM((COLS, SROW), f32), DMA],
        gathered, masked, row_basis, nearby,
    )
    return field, traction


def solution(mesh):
    in_specs = (
        P("dev", None, "sec", None),
        P("dev", None, "sec", None),
        P("sec", "dev"),
        P("dev", None, None),
        P("dev", None, None),
        P("dev"),
        P("dev", None, None),
        P("dev", None, None),
        P("dev", None, None),
        P("dev", None, None),
        P("dev", None),
    )
    out_specs = (P("dev", None, "sec", None), P("sec", "dev"))
    return jax.shard_map(
        block_steps, mesh=mesh, in_specs=in_specs, out_specs=out_specs, check_vma=False
    )
```
